256 devices in a mesh: dp: 4 (over y), ctx: 32 (over x_hi, z, core), head: 2 (over x_lo).
Axes of the slice: x: 4 (x_hi: 2, x_lo: 2; x = x_hi * 2 + x_lo), y: 4, z: 8, core: 2. Of those that a mesh axis runs over, the one named last changes fastest.
Arguments:
- queries: bfloat16 [4, 8192, 2048], P('dp', 'ctx', 'head'), may hold values from -35 to 35
- key_rows: bfloat16 [4, 8192, 2048], P('dp', 'ctx', 'head'), may hold values from -6 to 6
- value_rows: bfloat16 [4, 8192, 2048], P('dp', 'ctx', 'head'), may hold values from -6 to 6
- sink_logits: float32 [16], P('head'), may hold values from 4 to 9
- partner: int32 [3, 32], replicated, may hold values from 0 to 31, as said below
- block_pick: int32 [4, 3, 32], P('dp'), may hold values from 0 to 1
- out_grad: bfloat16 [4, 8192, 2048], P('dp', 'ctx', 'head'), may hold values from -18 to 18
Outputs:
- attention: bfloat16 [4, 8192, 2048], P('dp', 'ctx', 'head')
- query_grad: bfloat16 [4, 8192, 2048], P('dp', 'ctx', 'head')
- key_grad: bfloat16 [4, 8192, 2048], P('dp', 'ctx', 'head')
- value_grad: bfloat16 [4, 8192, 2048], P('dp', 'ctx', 'head')
- sink_grad: float32 [16], P('head')
The draws below stay inside these ranges and needn't reach their ends.
Inputs may be any that keep to these rules, and one draw needn't show every extreme that they name: partner[r, i] = i XOR partner[r, 0] for every round r, and partner[r, 0] is a power of two: each round pairs the indices of ctx that differ in one bit.
All inputs are finite; a program needn't handle non-finite values.
Results may differ from the reference program's by a relative error of at most 0.0093.
Values may be sent and summed in bfloat16 or wider, within the bound.
No kernel may reach another device: no remote copies, remote signals or barrier semaphores. Data moves between devices by JAX's collectives and lax.ppermute only.
A program may use at most 128 MiB of HBM per device.

```python
import math
import jax
import jax.numpy as jnp
from jax import lax

HEADS = 16
HD = 128
BLOCK = 128
ROUNDS = 3
TOK_DEV = 256
LENGTH = 8192
DOCS = 4
CTX_BITS = 5
N_CTX = 32


def joint_rows(key):
    full_shape = (DOCS, LENGTH, HEADS * HD)
    first_key = jax.random.fold_in(key, 101)
    second_key = jax.random.fold_in(key, 202)
    query_full = jnp.clip(jax.random.normal(first_key, full_shape, jnp.float32), -6.0, 6.0)
    key_full = jnp.clip(jax.random.normal(second_key, full_shape, jnp.float32), -6.0, 6.0)
    return (query_full, key_full)


def draw_queries(key, part):
    return joint_rows(key)[0].astype(jnp.bfloat16)


def draw_key_rows(key, part):
    return joint_rows(key)[1].astype(jnp.bfloat16)


def draw_out_grad(key, part):
    full_shape = (DOCS, LENGTH, HEADS * HD)
    position = jnp.arange(LENGTH, dtype=jnp.float32)[None, :, None] / max(LENGTH - 1, 1)
    document = jnp.arange(DOCS, dtype=jnp.float32)[:, None, None] / max(DOCS - 1, 1)
    base_draw = jnp.clip(jax.random.normal(key, full_shape, jnp.float32), -6.0, 6.0)
    rising = (1.0 + 2.0 * position) * (1.0 + 2.0 * document) / 3.0
    return (base_draw * rising).astype(jnp.bfloat16)


def draw_partner(key, part):
    bit_places = jax.random.randint(key, (ROUNDS, 1), 0, CTX_BITS, dtype=jnp.int32)
    xor_masks = jnp.left_shift(jnp.ones((ROUNDS, 1), jnp.int32), bit_places)
    return jnp.bitwise_xor(jnp.arange(N_CTX, dtype=jnp.int32)[None, :], xor_masks).astype(jnp.int32)


def plant(values, rng, low, high):
    longest = values.shape.index(max(values.shape))
    spots = []
    for shift in (0, 1):
        where = [jax.random.randint(jax.random.fold_in(rng, axis), (), 0, length) for axis, length in enumerate(values.shape)]
        where[longest] = (where[longest] + shift) % values.shape[longest]
        spots.append(tuple(where))
    return values.at[spots[0]].set(low).at[spots[1]].set(high)


def levels(own_key, extent, split, low, largest):
    def one(dim, parts):
        steps = jax.random.uniform(jax.random.fold_in(jax.random.fold_in(own_key, 6), dim), (parts,), jnp.float32, low / len(split), largest / len(split))
        return jnp.repeat(jnp.exp(steps), extent[dim] // parts).reshape((-1,) + (1,) * (len(extent) - dim - 1))

    gain = one(*split[0])
    for cut in split[1:]:
        gain = gain * one(*cut)
    return gain


def normal_values(stream_key, shape, scale, most, split=(), kind=jnp.bfloat16):
    values = scale * jax.random.normal(stream_key, shape, jnp.float32)
    if split:
        values = values * levels(stream_key, shape, split, -0.22, 0.18)
    return jnp.clip(values, -most, most).astype(kind)


def setup_inputs(seed: int = 0) -> dict:
    keys = jax.random.split(jax.random.key(seed), 8)
    queries = draw_queries(jax.random.fold_in(keys[7], 71), 0)
    key_rows = draw_key_rows(jax.random.fold_in(keys[7], 71), 0)
    value_rows = normal_values(keys[2], (DOCS, LENGTH, HEADS * HD), 1.0, 6.0, ((0, 4), (1, 32), (2, 2)))
    sink_logits = jnp.clip(4.0 + 5.0 * jax.random.uniform(keys[3], (HEADS,), jnp.float32) ** levels(keys[3], (HEADS,), ((0, 2),), -0.2, 0.2), 4.0, 9.0)
    partner = draw_partner(jax.random.fold_in(keys[7], 71), 0)
    block_pick = plant(jax.random.randint(keys[5], (DOCS, ROUNDS, N_CTX), 0, TOK_DEV // BLOCK), jax.random.fold_in(keys[5], 1), 0, (TOK_DEV // BLOCK) - 1).astype(jnp.int32)
    out_grad = draw_out_grad(jax.random.fold_in(keys[7], 71), 0)
    return dict(queries=queries, key_rows=key_rows, value_rows=value_rows, sink_logits=sink_logits, partner=partner, block_pick=block_pick, out_grad=out_grad)


def as_rounded(values):
    return lax.optimization_barrier(values.astype(jnp.bfloat16)).astype(jnp.float32)

def head_pass(query_one, key_one, value_one, grad_one, sink_one, pick_doc, partner):
    total_blocks = LENGTH // BLOCK
    shard_blocks = TOK_DEV // BLOCK
    scaling = HD ** (-0.5)
    query_blocks = query_one.reshape(total_blocks, BLOCK, HD).astype(jnp.float32)
    key_blocks = key_one.reshape(total_blocks, BLOCK, HD)
    value_blocks = value_one.reshape(total_blocks, BLOCK, HD)
    block_ids = jnp.arange(total_blocks, dtype=jnp.int32)
    owner = block_ids // shard_blocks
    random_cols = [(partner[number][owner] * shard_blocks + pick_doc[number][owner]).astype(jnp.int32) for number in range(ROUNDS)]
    slot_ids = jnp.stack([jnp.zeros_like(block_ids), jnp.full_like(block_ids, total_blocks - 1), jnp.clip(block_ids - 1, 0, total_blocks - 1), block_ids, jnp.clip(block_ids + 1, 0, total_blocks - 1)] + random_cols, axis=1).astype(jnp.int32)
    always = block_ids >= 0
    slot_valid = jnp.stack([always, always, block_ids != 1, always, block_ids != total_blocks - 2] + [always] * ROUNDS, axis=1)
    slot_keys = key_blocks[slot_ids].astype(jnp.float32)
    slot_values = value_blocks[slot_ids].astype(jnp.float32)
    scores = scaling * jnp.einsum('nqd,nskd->nqsk', query_blocks, slot_keys)
    scores = jnp.where(slot_valid[:, None, :, None], scores, -jnp.inf)
    row_top = jnp.maximum(sink_one, lax.optimization_barrier(jnp.max(scores, axis=(2, 3))))
    expo = jnp.exp(scores - row_top[:, :, None, None])
    row_total = jnp.exp(sink_one - row_top) + lax.optimization_barrier(jnp.sum(expo, axis=(2, 3)))
    weights = as_rounded(expo)
    regular_out = jnp.einsum('nqsk,nskd->nqd', weights, slot_values) / row_total[:, :, None]
    global_query = jnp.concatenate([query_one[:BLOCK], query_one[LENGTH - BLOCK:]], axis=0)
    global_scores = scaling * jnp.dot(global_query, key_one.T, preferred_element_type=jnp.float32)
    global_top = jnp.maximum(sink_one, lax.optimization_barrier(jnp.max(global_scores, axis=1)))
    global_expo = jnp.exp(global_scores - global_top[:, None])
    global_total = jnp.exp(sink_one - global_top) + lax.optimization_barrier(jnp.sum(global_expo, axis=1))
    global_out = jnp.dot(global_expo.astype(jnp.bfloat16), value_one, preferred_element_type=jnp.float32) / global_total[:, None]
    full_out = regular_out.reshape(LENGTH, HD)
    full_out = full_out.at[:BLOCK].set(global_out[:BLOCK]).at[LENGTH - BLOCK:].set(global_out[BLOCK:])
    attention = full_out.astype(jnp.bfloat16)
    grad_full = grad_one.astype(jnp.float32)
    row_delta = lax.optimization_barrier(jnp.sum(grad_full * attention.astype(jnp.float32), axis=1))
    row_blocks = jnp.arange(LENGTH) // BLOCK
    regular_rows = (row_blocks != 0) & (row_blocks != total_blocks - 1)
    grad_regular = jnp.where(regular_rows[:, None], grad_full, 0.0).reshape(total_blocks, BLOCK, HD)
    delta_regular = jnp.where(regular_rows, row_delta, 0.0).reshape(total_blocks, BLOCK)
    row_lse = row_top + jnp.log(row_total)
    probs = jnp.exp(scores - row_lse[:, :, None, None])
    prob_half = as_rounded(probs)
    prob_grad = jnp.einsum('nqd,nskd->nqsk', grad_regular, slot_values)
    score_grad = as_rounded(probs * (prob_grad - delta_regular[:, :, None, None]))
    query_regular = scaling * jnp.einsum('nqsk,nskd->nqd', score_grad, slot_keys)
    key_slots = scaling * jnp.einsum('nqsk,nqd->nskd', score_grad, query_blocks)
    value_slots = jnp.einsum('nqsk,nqd->nskd', prob_half, grad_regular)
    key_acc = jnp.zeros((total_blocks, BLOCK, HD), jnp.float32).at[slot_ids[:, :5]].add(key_slots[:, :5])
    value_acc = jnp.zeros((total_blocks, BLOCK, HD), jnp.float32).at[slot_ids[:, :5]].add(value_slots[:, :5])
    targets = slot_ids[:, 5:].reshape(N_CTX, shard_blocks, ROUNDS)[:, 0]
    key_random = as_rounded(key_slots[:, 5:].reshape(N_CTX, shard_blocks, ROUNDS, BLOCK, HD).sum(axis=1))
    value_random = as_rounded(value_slots[:, 5:].reshape(N_CTX, shard_blocks, ROUNDS, BLOCK, HD).sum(axis=1))
    key_acc = key_acc.at[targets].add(key_random)
    value_acc = value_acc.at[targets].add(value_random)
    global_lse = global_top + jnp.log(global_total)
    global_probs = jnp.exp(global_scores - global_lse[:, None])
    global_grad = jnp.concatenate([grad_one[:BLOCK], grad_one[LENGTH - BLOCK:]], axis=0)
    global_att = jnp.concatenate([attention[:BLOCK], attention[LENGTH - BLOCK:]], axis=0)
    global_delta = lax.optimization_barrier(jnp.sum(global_grad.astype(jnp.float32) * global_att.astype(jnp.float32), axis=1))
    global_dp = jnp.dot(global_grad, value_one.T, preferred_element_type=jnp.float32)
    global_ds = (global_probs * (global_dp - global_delta[:, None])).astype(jnp.bfloat16)
    global_dq = scaling * jnp.dot(global_ds, key_one, preferred_element_type=jnp.float32)
    key_total = key_acc.reshape(LENGTH, HD) + scaling * jnp.dot(global_ds.T, global_query, preferred_element_type=jnp.float32)
    value_total = value_acc.reshape(LENGTH, HD) + jnp.dot(global_probs.astype(jnp.bfloat16).T, global_grad, preferred_element_type=jnp.float32)
    query_total = query_regular.reshape(LENGTH, HD)
    query_total = query_total.at[:BLOCK].set(global_dq[:BLOCK]).at[LENGTH - BLOCK:].set(global_dq[BLOCK:])
    lse_rows = row_lse.reshape(LENGTH)
    lse_rows = lse_rows.at[:BLOCK].set(global_lse[:BLOCK]).at[LENGTH - BLOCK:].set(global_lse[BLOCK:])
    sink_term = -jnp.sum(jnp.exp(sink_one - lse_rows) * row_delta)
    return (attention, query_total.astype(jnp.bfloat16), key_total.astype(jnp.bfloat16), value_total.astype(jnp.bfloat16), sink_term)

def to_heads(matrix):
    return matrix.reshape(LENGTH, HEADS, HD).transpose(1, 0, 2)

def from_heads(tensor):
    return tensor.transpose(1, 0, 2).reshape(LENGTH, HEADS * HD)

def reference(queries, key_rows, value_rows, sink_logits, partner, block_pick, out_grad):

    def per_doc(items):
        query_doc, key_doc, value_doc, grad_doc, pick_doc = items

        def per_head(head_items):
            query_one, key_one, value_one, grad_one, sink_one = head_items
            return head_pass(query_one, key_one, value_one, grad_one, sink_one, pick_doc, partner)
        results = lax.map(per_head, (to_heads(query_doc), to_heads(key_doc), to_heads(value_doc), to_heads(grad_doc), sink_logits))
        return (from_heads(results[0]), from_heads(results[1]), from_heads(results[2]), from_heads(results[3]), results[4])
    outputs = lax.map(per_doc, (queries, key_rows, value_rows, out_grad, block_pick))
    sink_grad = lax.optimization_barrier(jnp.sum(outputs[4], axis=0)) / math.sqrt(DOCS * LENGTH)
    return (outputs[0], outputs[1], outputs[2], outputs[3], sink_grad)
```

```python
import math

import jax
import jax.numpy as jnp
from jax import lax
from jax.experimental import pallas as pl
from jax.experimental.pallas import tpu as pltpu
from jax.sharding import PartitionSpec as P

HD = 128
BLOCK = 128
ROUNDS = 3
BITS = 5
CTX = 32
INTERPRET = False
F32 = jnp.float32
BF16 = jnp.bfloat16
SCALING = HD ** (-0.5)
NT = (((1,), (1,)), ((), ()))
NN = (((1,), (0,)), ((), ()))
TN = (((0,), (0,)), ((), ()))


def dot(a, b, dims):
    return lax.dot_general(a, b, dims, preferred_element_type=F32)


def move(value, pairs):
    return lax.ppermute(value, "ctx", pairs)


def flip(value, bit):
    return move(value, [(i, i ^ (1 << bit)) for i in range(CTX)])


def spread_pairs(bit):
    mask = (2 << bit) - 1
    pairs = []
    for i in range(CTX):
        if i & mask == 0:
            pairs.append((i, i | (1 << bit)))
        if i & mask == mask:
            pairs.append((i, i & ~(1 << bit)))
    return pairs


def collect_pairs(bit):
    return [(j, i) for i, j in spread_pairs(bit)]


def routed(package, bit_place):
    return lax.switch(
        bit_place, [lambda value, bit=bit: flip(value, bit) for bit in range(BITS)], package
    )


def regular_kernel(
    flags, sink, q, g, k, v, prev, nxt, mine, other, ra, rb, rc,
    att, dq, dk_own, dv_own, d_prev, d_next, d_mine, d_other, d_ra, d_rb, d_rc, sink_out,
):
    sink_h = sink[pl.program_id(0)]
    ends = (flags[0] == 1, flags[1] == 1)
    keys = [prev[0], k[:BLOCK], k[BLOCK:], nxt[0], mine[1], other[1], ra[0], rb[0], rc[0]]
    vals = [prev[1], v[:BLOCK], v[BLOCK:], nxt[1], mine[2], other[2], ra[1], rb[1], rc[1]]
    totals_k = [None] * 9
    totals_v = [None] * 9
    sink_sum = jnp.zeros((1, 1), F32)
    for n in range(2):
        rows = slice(n * BLOCK, (n + 1) * BLOCK)
        slots = [n, n + 1, n + 2, 4, 5, 6, 7, 8]
        k_all = jnp.concatenate([keys[j] for j in slots], axis=0)
        v_all = jnp.concatenate([vals[j] for j in slots], axis=0)
        qn = q[rows]
        gn = jnp.where(ends[n], jnp.zeros((BLOCK, HD), BF16), g[rows])
        s = dot(qn, k_all, NT) * SCALING
        parts = [s[:, j * BLOCK : (j + 1) * BLOCK] for j in range(8)]
        masked = 0 if n == 1 else 2
        parts[masked] = jnp.where(ends[1 - n], -jnp.inf, parts[masked])
        s = jnp.concatenate(parts, axis=1)
        top = jnp.maximum(jnp.max(s, axis=1, keepdims=True), sink_h)
        e = jnp.exp(s - top)
        sink_e = jnp.exp(sink_h - top)
        total = sink_e + jnp.sum(e, axis=1, keepdims=True)
        inverse = 1.0 / total
        acc = dot(e.astype(BF16), v_all, NN)
        half = (acc * inverse).astype(BF16)
        att[rows] = half
        delta = jnp.sum(gn.astype(F32) * half.astype(F32), axis=1, keepdims=True)
        sink_sum = sink_sum + jnp.sum(sink_e * inverse * delta, axis=0, keepdims=True)
        p = e * inverse
        dp = dot(gn, v_all, NT)
        ds = (p * (dp - delta)).astype(BF16)
        ph = p.astype(BF16)
        dq[rows] = (dot(ds, k_all, NN) * SCALING).astype(BF16)
        dk = dot(ds, qn, TN) * SCALING
        dv = dot(ph, gn, TN)
        for j, slot in enumerate(slots):
            piece = slice(j * BLOCK, (j + 1) * BLOCK)
            totals_k[slot] = dk[piece] if totals_k[slot] is None else totals_k[slot] + dk[piece]
            totals_v[slot] = dv[piece] if totals_v[slot] is None else totals_v[slot] + dv[piece]
    for n in range(2):
        rows = slice(n * BLOCK, (n + 1) * BLOCK)
        dk_own[rows] = totals_k[n + 1]
        dv_own[rows] = totals_v[n + 1]
    for slot, out in ((0, d_prev), (3, d_next), (4, d_mine), (5, d_other), (6, d_ra), (7, d_rb), (8, d_rc)):
        out[0] = totals_k[slot].astype(BF16)
        out[1] = totals_v[slot].astype(BF16)
    sink_out[0] = jnp.broadcast_to(sink_sum, (8, HD))


def stats_kernel(k, v, mine, other, stats):
    gq = jnp.concatenate([mine[0], other[0]], axis=0)
    gg = jnp.concatenate([mine[3], other[3]], axis=0)
    s = dot(k[...], gq, NT) * SCALING
    top = jnp.max(s, axis=0, keepdims=True)
    e = jnp.exp(s - top)
    dp = dot(v[...], gg, NT)
    stats[0, 0:1] = top
    stats[0, 1:2] = jnp.sum(e, axis=0, keepdims=True)
    stats[0, 2:3] = jnp.sum(e * dp, axis=0, keepdims=True)


def global_kernel(k, v, mine, other, stats, d_mine, d_other, dk_own, dv_own):
    gq = jnp.concatenate([mine[0], other[0]], axis=0)
    gg = jnp.concatenate([mine[3], other[3]], axis=0)
    kk = k[...]
    vv = v[...]
    lse = stats[0, 0:1]
    delta = stats[0, 1:2]
    p = jnp.exp(dot(kk, gq, NT) * SCALING - lse)
    ph = p.astype(BF16)
    ds = (p * (dot(vv, gg, NT) - delta)).astype(BF16)
    acc = dot(ph, vv, TN).astype(BF16)
    dq = (dot(ds, kk, TN) * SCALING).astype(BF16)
    d_mine[0] = acc[:BLOCK]
    d_mine[1] = dq[:BLOCK]
    d_other[0] = acc[BLOCK:]
    d_other[1] = dq[BLOCK:]
    dk_own[...] = dot(ds, gq, NN) * SCALING
    dv_own[...] = dot(ph, gg, NN)


def final_kernel(
    flags, att_r, dq_r, dk_a, dv_a, dk_b, dv_b, above, below, ra, rb, rc,
    sum_kv, got_kv, sum_aq, got_aq, att, dq, dk, dv,
):
    root_kv = sum_kv[...].astype(F32) + got_kv[...].astype(F32)
    root_aq = sum_aq[...].astype(F32) + got_aq[...].astype(F32)
    for n in range(2):
        rows = slice(n * BLOCK, (n + 1) * BLOCK)
        is_root = flags[n] == 1
        att[rows] = jnp.where(is_root, root_aq[0].astype(BF16), att_r[rows])
        dq[rows] = jnp.where(is_root, root_aq[1].astype(BF16), dq_r[rows])
        edge = below if n == 0 else above
        for part, (out, first, second) in enumerate(((dk, dk_a, dk_b), (dv, dv_a, dv_b))):
            value = first[rows] + second[rows] + edge[part].astype(F32)
            value = value + jnp.where(is_root, root_kv[part], 0.0)
            for r, back in enumerate((ra, rb, rc)):
                value = value + jnp.where(flags[2 + r] == n, back[part].astype(F32), 0.0)
            out[rows] = value.astype(BF16)


def rows_spec(count=2 * BLOCK):
    return pl.BlockSpec((count, HD), lambda h: (0, h))


def stack_spec(depth):
    return pl.BlockSpec((depth, BLOCK, HD), lambda h: (0, 0, h))


def smem_spec():
    return pl.BlockSpec(memory_space=pltpu.SMEM)


def stat_spec(count, width):
    return pl.BlockSpec((1, count, width), lambda h: (h, 0, 0))


def shaped(shape, dtype):
    return jax.ShapeDtypeStruct(shape, dtype)


def add_half(a, b):
    return (a.astype(F32) + b.astype(F32)).astype(BF16)


def merge(parts):
    top = parts[0][:, 0]
    for part in parts[1:]:
        top = jnp.maximum(top, part[:, 0])
    total = 0.0
    weighted = 0.0
    for part in parts:
        factor = jnp.exp(part[:, 0] - top)
        total = total + part[:, 1] * factor
        weighted = weighted + part[:, 2] * factor
    return jnp.stack([top, total, weighted], axis=1)


def body(queries, key_rows, value_rows, sink_logits, partner, block_pick, out_grad):
    q, k, v, g = queries[0], key_rows[0], value_rows[0], out_grad[0]
    tokens, width = q.shape
    heads = width // HD
    place = lax.axis_index("ctx")
    core = place % 2
    is_first = (place == 0).astype(jnp.int32)
    is_last = (place == CTX - 1).astype(jnp.int32)

    def call(kernel, ins, outs, scalars=0):
        return pl.pallas_call(
            kernel,
            grid=(heads,),
            in_specs=[smem_spec()] * scalars + ins,
            out_specs=[spec for spec, _ in outs],
            out_shape=[shape for _, shape in outs],
            interpret=INTERPRET,
        )

    masks = partner[:, 0]
    bit_places = sum((masks >= (1 << b)).astype(jnp.int32) for b in range(1, BITS))
    partner_place = jnp.bitwise_xor(place, masks)
    ctx_match = jnp.arange(CTX)[None, :] == partner_place[:, None]
    wanted = jnp.sum(jnp.where(ctx_match, block_pick[0], 0), axis=1)

    def cut(array, block):
        return lax.dynamic_slice_in_dim(array, block * BLOCK, BLOCK, 0)

    mine = jnp.stack([cut(array, is_last) for array in (q, k, v, g)])
    low_pair = jnp.stack([k[:BLOCK], v[:BLOCK]])
    high_pair = jnp.stack([k[tokens - BLOCK :], v[tokens - BLOCK :]])
    packages = [jnp.stack([cut(k, wanted[r]), cut(v, wanted[r])]) for r in range(ROUNDS)]
    up = [(i, i + 1) for i in range(CTX - 1)]
    down = [(i + 1, i) for i in range(CTX - 1)]
    fetched = []
    for step, bit in enumerate((4, 3, 2, 1)):
        got = move(mine, spread_pairs(bit))
        if step < ROUNDS:
            fetched.append(routed(packages[step], bit_places[step]))
        mask = (2 << bit) - 1
        low = place & mask
        takes = (low == (1 << bit)) | (low == mask - (1 << bit))
        mine = jnp.where(takes, got, mine)
    prev = move(high_pair, up)
    nxt = move(low_pair, down)
    other = flip(mine, 0)

    (stats,) = call(
        stats_kernel,
        [rows_spec()] * 2 + [stack_spec(4)] * 2,
        [(stat_spec(3, 2 * BLOCK), shaped((heads, 3, 2 * BLOCK), F32))],
    )(k, v, mine, other)
    ring = []
    for offset in range(1, 8):
        pairs = [
            (i, (i & 17) | ((((i >> 1) + offset) & 7) << 1)) for i in range(CTX)
        ]
        ring.append(move(stats, pairs))
    stats = merge([stats] + ring)
    across = flip(stats, 4)
    swapped = jnp.concatenate([stats[:, :, BLOCK:], stats[:, :, :BLOCK]], axis=2)
    beside = flip(swapped, 0)
    diagonal = move(swapped, [(i, i ^ 17) for i in range(CTX)])
    stats = merge([stats, across, beside, diagonal])
    sink_column = sink_logits[:, None]
    top = jnp.maximum(stats[:, 0], sink_column)
    factor = jnp.exp(stats[:, 0] - top)
    total = jnp.exp(sink_column - top) + stats[:, 1] * factor
    lse = top + jnp.log(total)
    delta = stats[:, 2] * factor / total
    global_sink = jnp.sum(jnp.exp(sink_column - lse) * delta, axis=1)
    lse_delta = jnp.stack([lse, delta], axis=1)

    pair = (stack_spec(2), shaped((2, BLOCK, width), BF16))
    half_rows = (rows_spec(), shaped((tokens, width), BF16))
    full_rows = (rows_spec(), shaped((tokens, width), F32))
    flags = jnp.stack([is_first, is_last])
    (att_r, dq_r, dk_a, dv_a, d_prev, d_next, kv_mine, kv_other, *d_random, sink_part) = call(
        regular_kernel,
        [rows_spec()] * 4 + [stack_spec(2)] * 2 + [stack_spec(4)] * 2 + [stack_spec(2)] * 3,
        [half_rows] * 2 + [full_rows] * 2 + [pair] * 7
        + [(stat_spec(8, HD), shaped((heads, 8, HD), F32))],
        2,
    )(flags, sink_logits, q, g, k, v, prev, nxt, mine, other, *fetched)

    (aq_mine, aq_other, dk_b, dv_b) = call(
        global_kernel,
        [rows_spec()] * 2 + [stack_spec(4)] * 2 + [stat_spec(2, 2 * BLOCK)],
        [pair] * 2 + [full_rows] * 2,
    )(k, v, mine, other, lse_delta)

    above = move(d_prev, down)
    below = move(d_next, up)
    sink_row = sink_part[:, 0]
    kv_sum = add_half(kv_mine, flip(kv_other, 0))
    aq_sum = add_half(aq_mine, flip(aq_other, 0))
    sink_row = sink_row + flip(sink_row, 0)
    returned = []
    for step, bit in enumerate((1, 2, 3)):
        kv_got = move(kv_sum, collect_pairs(bit))
        aq_got = move(aq_sum, collect_pairs(bit))
        sink_got = flip(sink_row, bit)
        returned.append(routed(d_random[step], bit_places[step]))
        kv_sum = add_half(kv_sum, kv_got)
        aq_sum = add_half(aq_sum, aq_got)
        sink_row = sink_row + sink_got
    kv_got = move(kv_sum, collect_pairs(4))
    aq_got = move(aq_sum, collect_pairs(4))
    sink_row = sink_row + flip(sink_row, 4) + global_sink[:, None]
    docs = lax.axis_size("dp")
    others = [
        lax.ppermute(sink_row, "dp", [(i, (i + step) % docs) for i in range(docs)])
        for step in range(1, docs)
    ]
    for value in others:
        sink_row = sink_row + value
    sink_grad = -sink_row[:, 0] / math.sqrt(docs * CTX * tokens)

    flags = jnp.concatenate([flags, wanted.astype(jnp.int32)])
    outs = call(
        final_kernel,
        [rows_spec()] * 6 + [stack_spec(2)] * 9,
        [half_rows] * 4,
        1,
    )(flags, att_r, dq_r, dk_a, dv_a, dk_b, dv_b, above, below, *returned, kv_sum, kv_got, aq_sum, aq_got)
    attention, query_grad, key_grad, value_grad = [out[None] for out in outs]
    return (attention, query_grad, key_grad, value_grad, sink_grad)


def solution(mesh):
    whole = P("dp", "ctx", "head")
    return jax.shard_map(
        body,
        mesh=mesh,
        in_specs=(whole, whole, whole, P("head"), P(), P("dp", None, None), whole),
        out_specs=(whole, whole, whole, whole, P("head")),
        check_vma=False,
    )
```

```python
import math

import jax
import jax.numpy as jnp
from jax import lax
from jax.experimental import pallas as pl
from jax.experimental.pallas import tpu as pltpu
from jax.sharding import PartitionSpec as P


HD = 128
BLOCK = 128
ROUNDS = 3
BITS = 5
CTX = 32
INTERPRET = False
F32 = jnp.float32
BF16 = jnp.bfloat16
SCALING = HD ** (-0.5)
NT = (((1,), (1,)), ((), ()))
NN = (((1,), (0,)), ((), ()))
TN = (((0,), (0,)), ((), ()))


def dot(a, b, dims):
    return lax.dot_general(a, b, dims, preferred_element_type=F32)


def move(value, pairs):
    return lax.ppermute(value, "ctx", pairs)


def flip(value, bit):
    return move(value, [(i, i ^ (1 << bit)) for i in range(CTX)])


def spread_pairs(bit):
    mask = (2 << bit) - 1
    pairs = []
    for i in range(CTX):
        if i & mask == 0:
            pairs.append((i, i | (1 << bit)))
        if i & mask == mask:
            pairs.append((i, i & ~(1 << bit)))
    return pairs


def collect_pairs(bit):
    return [(j, i) for i, j in spread_pairs(bit)]


def routed(package, bit_place):
    return lax.switch(
        bit_place, [lambda value, bit=bit: flip(value, bit) for bit in range(BITS)], package
    )


def regular_kernel(
    flags, sink, q, g, k, v, prev, nxt, mine, other, ra, rb, rc,
    *refs, first_head,
):
    att, dq, dk_own, dv_own, d_prev, d_next, d_mine, d_other, d_ra, d_rb, d_rc, sink_out = refs[-12:]
    sink_h = sink[pl.program_id(0) + first_head]
    ends = (flags[0] == 1, flags[1] == 1)
    keys = [prev[0], k[:BLOCK], k[BLOCK:], nxt[0], mine[1], other[1], ra[0], rb[0], rc[0]]
    vals = [prev[1], v[:BLOCK], v[BLOCK:], nxt[1], mine[2], other[2], ra[1], rb[1], rc[1]]
    totals_k = [None] * 9
    totals_v = [None] * 9
    sink_sum = jnp.zeros((1, 1), F32)
    for n in range(2):
        rows = slice(n * BLOCK, (n + 1) * BLOCK)
        slots = [n, n + 1, n + 2, 4, 5, 6, 7, 8]
        k_all = jnp.concatenate([keys[j] for j in slots], axis=0)
        v_all = jnp.concatenate([vals[j] for j in slots], axis=0)
        qn = q[rows]
        gn = jnp.where(ends[n], jnp.zeros((BLOCK, HD), BF16), g[rows])
        s = dot(qn, k_all, NT) * SCALING
        parts = [s[:, j * BLOCK : (j + 1) * BLOCK] for j in range(8)]
        masked = 0 if n == 1 else 2
        parts[masked] = jnp.where(ends[1 - n], -jnp.inf, parts[masked])
        s = jnp.concatenate(parts, axis=1)
        top = jnp.maximum(jnp.max(s, axis=1, keepdims=True), sink_h)
        e = jnp.exp(s - top)
        sink_e = jnp.exp(sink_h - top)
        total = sink_e + jnp.sum(e, axis=1, keepdims=True)
        inverse = 1.0 / total
        acc = dot(e.astype(BF16), v_all, NN)
        half = (acc * inverse).astype(BF16)
        att[rows] = half
        delta = jnp.sum(gn.astype(F32) * half.astype(F32), axis=1, keepdims=True)
        sink_sum = sink_sum + jnp.sum(sink_e * inverse * delta, axis=0, keepdims=True)
        p = e * inverse
        dp = dot(gn, v_all, NT)
        ds = (p * (dp - delta)).astype(BF16)
        ph = p.astype(BF16)
        dq[rows] = (dot(ds, k_all, NN) * SCALING).astype(BF16)
        dk = dot(ds, qn, TN) * SCALING
        dv = dot(ph, gn, TN)
        for j, slot in enumerate(slots):
            piece = slice(j * BLOCK, (j + 1) * BLOCK)
            totals_k[slot] = dk[piece] if totals_k[slot] is None else totals_k[slot] + dk[piece]
            totals_v[slot] = dv[piece] if totals_v[slot] is None else totals_v[slot] + dv[piece]
    for n in range(2):
        rows = slice(n * BLOCK, (n + 1) * BLOCK)
        dk_own[rows] = totals_k[n + 1]
        dv_own[rows] = totals_v[n + 1]
    for slot, out in ((0, d_prev), (3, d_next), (4, d_mine), (5, d_other), (6, d_ra), (7, d_rb), (8, d_rc)):
        out[0] = totals_k[slot].astype(BF16)
        out[1] = totals_v[slot].astype(BF16)
    sink_out[0] = jnp.broadcast_to(sink_sum, (8, HD))


def stats_kernel(k, v, mine, other, stats):
    gq = jnp.concatenate([mine[0], other[0]], axis=0)
    gg = jnp.concatenate([mine[3], other[3]], axis=0)
    s = dot(k[...], gq, NT) * SCALING
    top = jnp.max(s, axis=0, keepdims=True)
    e = jnp.exp(s - top)
    dp = dot(v[...], gg, NT)
    stats[0, 0:1] = top
    stats[0, 1:2] = jnp.sum(e, axis=0, keepdims=True)
    stats[0, 2:3] = jnp.sum(e * dp, axis=0, keepdims=True)


def global_kernel(k, v, mine, other, stats, dk_in, dv_in, d_mine, d_other, dk_out, dv_out):
    gq = jnp.concatenate([mine[0], other[0]], axis=0)
    gg = jnp.concatenate([mine[3], other[3]], axis=0)
    kk = k[...]
    vv = v[...]
    lse = stats[0, 0:1]
    delta = stats[0, 1:2]
    p = jnp.exp(dot(kk, gq, NT) * SCALING - lse)
    ph = p.astype(BF16)
    ds = (p * (dot(vv, gg, NT) - delta)).astype(BF16)
    acc = dot(ph, vv, TN).astype(BF16)
    dq = (dot(ds, kk, TN) * SCALING).astype(BF16)
    d_mine[0] = acc[:BLOCK]
    d_mine[1] = dq[:BLOCK]
    d_other[0] = acc[BLOCK:]
    d_other[1] = dq[BLOCK:]
    dk_out[...] = dk_in[...] + dot(ds, gq, NN) * SCALING
    dv_out[...] = dv_in[...] + dot(ph, gg, NN)


def pair_kernel(flags, dk_in, dv_in, above, below, ra, rb, rc, sum_kv, got_kv, dk, dv):
    root = sum_kv[...].astype(F32) + got_kv[...].astype(F32)
    for n in range(2):
        rows = slice(n * BLOCK, (n + 1) * BLOCK)
        is_root = flags[n] == 1
        edge = below if n == 0 else above
        for part, (out, first) in enumerate(((dk, dk_in), (dv, dv_in))):
            value = first[rows] + edge[part].astype(F32)
            value = value + jnp.where(is_root, root[part], 0.0)
            for r, back in enumerate((ra, rb, rc)):
                value = value + jnp.where(flags[2 + r] == n, back[part].astype(F32), 0.0)
            out[rows] = value.astype(BF16)


def root_kernel(flags, sum_aq, got_aq, att_in, dq_in, att, dq, rows, sems):
    del att_in, dq_in
    is_last = flags[1] == 1

    @pl.when((flags[0] == 1) | is_last)
    def _():
        rows[...] = (sum_aq[...].astype(F32) + got_aq[...].astype(F32)).astype(BF16)
        start = pl.multiple_of(jnp.where(is_last, BLOCK, 0), BLOCK)
        copies = [
            pltpu.make_async_copy(rows.at[i], out.at[pl.ds(start, BLOCK)], sems.at[i])
            for i, out in enumerate((att, dq))
        ]
        for copy in copies:
            copy.start()
        for copy in copies:
            copy.wait()


def rows_spec(first=0):
    return pl.BlockSpec((2 * BLOCK, HD), lambda h: (0, h + first))


def stack_spec(depth, first=0):
    return pl.BlockSpec((depth, BLOCK, HD), lambda h: (0, 0, h + first))


def stat_spec(count, width, first=0):
    return pl.BlockSpec((1, count, width), lambda h: (h + first, 0, 0))


def smem_spec():
    return pl.BlockSpec(memory_space=pltpu.SMEM)


def shaped(shape, dtype):
    return jax.ShapeDtypeStruct(shape, dtype)


def add_half(a, b):
    return (a.astype(F32) + b.astype(F32)).astype(BF16)


def merge(a, b):
    top = jnp.maximum(a[:, 0], b[:, 0])
    fa = jnp.exp(a[:, 0] - top)
    fb = jnp.exp(b[:, 0] - top)
    return jnp.stack(
        [top, a[:, 1] * fa + b[:, 1] * fb, a[:, 2] * fa + b[:, 2] * fb], axis=1
    )


PARTS = ((0, 2), (2, 2), (4, 2), (6, 1), (7, 1))
STAT_BITS = (3, 2, 4, 1, 0)


def device_body(queries, key_rows, value_rows, sink_logits, partner, block_pick, out_grad):
    q, k, v, g = queries[0], key_rows[0], value_rows[0], out_grad[0]
    tokens, width = q.shape
    heads = width // HD
    place = lax.axis_index("ctx")
    is_first = (place == 0).astype(jnp.int32)
    is_last = (place == CTX - 1).astype(jnp.int32)

    def call(kernel, ins, outs, scalars=0, grid=None, **more):
        return lambda *operands: pl.pallas_call(
            kernel,
            grid=(heads if grid is None else grid,),
            in_specs=[smem_spec()] * scalars + ins,
            out_specs=[spec for spec, _ in outs],
            out_shape=[shape for _, shape in outs],
            interpret=INTERPRET,
            **more,
        )(*operands)

    masks = partner[:, 0]
    bit_places = sum((masks >= (1 << b)).astype(jnp.int32) for b in range(1, BITS))
    partner_place = jnp.bitwise_xor(place, masks)
    ctx_match = jnp.arange(CTX)[None, :] == partner_place[:, None]
    wanted = jnp.sum(jnp.where(ctx_match, block_pick[0], 0), axis=1)

    def cut(array, block):
        return lax.dynamic_slice_in_dim(array, block * BLOCK, BLOCK, 0)

    up = [(i, i + 1) for i in range(CTX - 1)]
    down = [(i + 1, i) for i in range(CTX - 1)]
    prev = move(jnp.stack([k[tokens - BLOCK :], v[tokens - BLOCK :]]), up)
    nxt = move(jnp.stack([k[:BLOCK], v[:BLOCK]]), down)
    mine = jnp.stack([cut(array, is_last) for array in (q, k, v, g)])
    packages = [jnp.stack([cut(k, wanted[r]), cut(v, wanted[r])]) for r in range(ROUNDS)]
    fetched = []
    for step, bit in enumerate((4, 3, 2, 1)):
        got = move(mine, spread_pairs(bit))
        if step < ROUNDS:
            fetched.append(routed(packages[step], bit_places[step]))
        mask = (2 << bit) - 1
        low = place & mask
        takes = (low == (1 << bit)) | (low == mask - (1 << bit))
        mine = jnp.where(takes, got, mine)
    other = flip(mine, 0)

    (stats,) = call(
        stats_kernel,
        [rows_spec()] * 2 + [stack_spec(4)] * 2,
        [(stat_spec(3, 2 * BLOCK), shaped((heads, 3, 2 * BLOCK), F32))],
    )(k, v, mine, other)
    for bit in STAT_BITS:
        sent = stats if bit else jnp.concatenate([stats[:, :, BLOCK:], stats[:, :, :BLOCK]], axis=2)
        arrived = flip(sent, bit)
        stats = merge(stats, arrived)
    sink_column = sink_logits[:, None]
    top = jnp.maximum(stats[:, 0], sink_column)
    factor = jnp.exp(stats[:, 0] - top)
    total = jnp.exp(sink_column - top) + stats[:, 1] * factor
    lse = top + jnp.log(total)
    delta = stats[:, 2] * factor / total
    global_sink = jnp.sum(jnp.exp(sink_column - lse) * delta, axis=1)
    lse_delta = jnp.stack([lse, delta], axis=1)

    pair = shaped((2, BLOCK, width), BF16)
    half_rows = shaped((tokens, width), BF16)
    full_rows = shaped((tokens, width), F32)
    ends = jnp.stack([is_first, is_last])
    shapes = [half_rows] * 2 + [full_rows] * 2 + [pair] * 7 + [shaped((heads, 8, HD), F32)]
    inputs = (ends, sink_logits, q, g, k, v, prev, nxt, mine, other, *fetched)
    kept = []
    parts = PARTS if heads == 8 else ((0, heads),)
    for first, count in parts:
        specs = [rows_spec(first)] * 4 + [stack_spec(2, first)] * 7 + [stat_spec(8, HD, first)]
        kept = call(
            lambda *refs, first=first: regular_kernel(*refs, first_head=first),
            [rows_spec(first)] * 4 + [stack_spec(2, first)] * 2 + [stack_spec(4, first)] * 2
            + [stack_spec(2, first)] * 3 + [pl.BlockSpec(memory_space=pl.ANY)] * len(kept),
            list(zip(specs, shapes)),
            2,
            count,
            input_output_aliases={len(inputs) + i: i for i in range(len(kept))},
        )(*inputs, *kept)
    (att_r, dq_r, dk_a, dv_a, d_prev, d_next, kv_mine, kv_other, *d_random, sink_part) = kept

    (aq_mine, aq_other, dk_b, dv_b) = call(
        global_kernel,
        [rows_spec()] * 2 + [stack_spec(4)] * 2 + [stat_spec(2, 2 * BLOCK)] + [rows_spec()] * 2,
        [(stack_spec(2), pair)] * 2 + [(rows_spec(), full_rows)] * 2,
        input_output_aliases={5: 2, 6: 3},
    )(k, v, mine, other, lse_delta, dk_a, dv_a)

    above = move(d_prev, down)
    below = move(d_next, up)
    sink_row = sink_part[:, 0]
    kv_got = flip(kv_other, 0)
    sink_got = flip(sink_row, 0)
    aq_got = flip(aq_other, 0)
    kv_sum = add_half(kv_mine, kv_got)
    aq_sum = add_half(aq_mine, aq_got)
    sink_row = sink_row + sink_got
    returned = []
    for step, bit in enumerate((1, 2, 3, 4)):
        kv_got = move(kv_sum, collect_pairs(bit))
        sink_got = flip(sink_row, bit)
        aq_got = move(aq_sum, collect_pairs(bit))
        if step < ROUNDS:
            returned.append(routed(d_random[step], bit_places[step]))
            kv_sum = add_half(kv_sum, kv_got)
            aq_sum = add_half(aq_sum, aq_got)
        sink_row = sink_row + sink_got
    sink_row = sink_row + global_sink[:, None]
    docs = lax.axis_size("dp")
    others = []
    for step in range(1, docs):
        others.append(lax.ppermute(sink_row, "dp", [(i, (i + step) % docs) for i in range(docs)]))
    for value in others:
        sink_row = sink_row + value
    sink_grad = -sink_row[:, 0] / math.sqrt(docs * CTX * tokens)

    flags = jnp.concatenate([ends, wanted.astype(jnp.int32)])
    key_grad, value_grad = call(
        pair_kernel, [rows_spec()] * 2 + [stack_spec(2)] * 7, [(rows_spec(), half_rows)] * 2, 1
    )(flags, dk_b, dv_b, above, below, *returned, kv_sum, kv_got)
    whole = pl.BlockSpec((2, BLOCK, width), lambda h: (0, 0, 0))
    anywhere = pl.BlockSpec(memory_space=pl.ANY)
    attention, query_grad = call(
        root_kernel,
        [whole] * 2 + [anywhere] * 2,
        [(anywhere, half_rows)] * 2,
        1,
        1,
        input_output_aliases={3: 0, 4: 1},
        scratch_shapes=[pltpu.VMEM((2, BLOCK, width), BF16), pltpu.SemaphoreType.DMA((2,))],
    )(ends, aq_sum, aq_got, att_r, dq_r)
    return (attention[None], query_grad[None], key_grad[None], value_grad[None], sink_grad)


def solution(mesh):
    whole = P("dp", "ctx", "head")
    return jax.shard_map(
        device_body,
        mesh=mesh,
        in_specs=(whole, whole, whole, P("head"), P(), P("dp", None, None), whole),
        out_specs=(whole, whole, whole, whole, P("head")),
        check_vma=False,
    )
```

```python
import math

import jax
import jax.numpy as jnp
from jax import lax
from jax.experimental import pallas as pl
from jax.experimental.pallas import tpu as pltpu
from jax.sharding import PartitionSpec as P


HD = 128
BLOCK = 128
ROUNDS = 3
BITS = 5
CTX = 32
INTERPRET = False
F32 = jnp.float32
BF16 = jnp.bfloat16
SCALING = HD ** (-0.5)
LOG2E = math.log2(math.e)
EXP2 = SCALING * LOG2E
NT = (((1,), (1,)), ((), ()))
NN = (((1,), (0,)), ((), ()))
TN = (((0,), (0,)), ((), ()))


def dot(a, b, dims):
    return lax.dot_general(a, b, dims, preferred_element_type=F32)


def move(value, pairs):
    return lax.ppermute(value, "ctx", pairs)


def flip(value, bit):
    return move(value, [(i, i ^ (1 << bit)) for i in range(CTX)])


def spread_pairs(bit):
    mask = (2 << bit) - 1
    pairs = []
    for i in range(CTX):
        if i & mask == 0:
            pairs.append((i, i | (1 << bit)))
        if i & mask == mask:
            pairs.append((i, i & ~(1 << bit)))
    return pairs


def collect_pairs(bit):
    return [(j, i) for i, j in spread_pairs(bit)]


def routed(package, bit_place):
    return lax.switch(
        bit_place, [lambda value, bit=bit: flip(value, bit) for bit in range(BITS)], package
    )


def regular_kernel(
    flags, sink, q, g, k, v, prev, nxt, mine, other, ra, rb, rc,
    *refs, first_head,
):
    att, dq, dk_own, dv_own, d_prev, d_next, d_mine, d_other, d_ra, d_rb, d_rc, sink_out = refs[-12:]
    sink_h = sink[pl.program_id(0) + first_head] * (1.0 / SCALING)
    ends = (flags[0] == 1, flags[1] == 1)
    zero = jnp.zeros((BLOCK, HD), BF16)
    halves = (slice(0, BLOCK), slice(BLOCK, 2 * BLOCK))
    qq = q[...]
    gg = jnp.concatenate([jnp.where(ends[n], zero, g[halves[n]]) for n in range(2)], axis=0)
    k_shared = jnp.concatenate([mine[1], other[1], ra[0], rb[0], rc[0]], axis=0)
    v_shared = jnp.concatenate([mine[2], other[2], ra[1], rb[1], rc[1]], axis=0)
    k_line = jnp.concatenate([prev[0], k[...], nxt[0]], axis=0)
    v_line = jnp.concatenate([prev[1], v[...], nxt[1]], axis=0)
    near = [slice(n * BLOCK, (n + 3) * BLOCK) for n in range(2)]

    def joined(make):
        return jnp.concatenate([make(n) for n in range(2)], axis=0)

    def near_scores(n):
        s = dot(qq[halves[n]], k_line[near[n]], NT)
        parts = [s[:, j * BLOCK : (j + 1) * BLOCK] for j in range(3)]
        masked = 0 if n == 1 else 2
        parts[masked] = jnp.where(ends[1 - n], -jnp.inf, parts[masked])
        return jnp.concatenate(parts, axis=1)

    s_far = dot(qq, k_shared, NT)
    s_near = joined(near_scores)
    top = jnp.maximum(jnp.max(s_far, axis=1, keepdims=True), jnp.max(s_near, axis=1, keepdims=True))
    top = jnp.maximum(top, sink_h)
    e_far = jnp.exp2((s_far - top) * EXP2)
    e_near = jnp.exp2((s_near - top) * EXP2)
    sink_e = jnp.exp2((sink_h - top) * EXP2)
    total = sink_e + jnp.sum(e_far, axis=1, keepdims=True) + jnp.sum(e_near, axis=1, keepdims=True)
    inverse = 1.0 / total
    h_far = e_far.astype(BF16)
    h_near = e_near.astype(BF16)
    acc = dot(h_far, v_shared, NN) + joined(lambda n: dot(h_near[halves[n]], v_line[near[n]], NN))
    half = (acc * inverse).astype(BF16)
    att[...] = half
    delta = jnp.sum(gg.astype(F32) * half.astype(F32), axis=1, keepdims=True)
    sink_sum = jnp.sum(sink_e * inverse * delta, axis=0, keepdims=True)
    sink_out[0] = jnp.broadcast_to(sink_sum, (8, HD))
    p_far = e_far * inverse
    p_near = e_near * inverse
    ds_far = (p_far * (dot(gg, v_shared, NT) - delta)).astype(BF16)
    dp_near = joined(lambda n: dot(gg[halves[n]], v_line[near[n]], NT))
    ds_near = (p_near * (dp_near - delta)).astype(BF16)
    p_far = p_far.astype(BF16)
    p_near = p_near.astype(BF16)
    back = dot(ds_far, k_shared, NN) + joined(lambda n: dot(ds_near[halves[n]], k_line[near[n]], NN))
    dq[...] = (back * SCALING).astype(BF16)
    for part, far, close, rows, scale, own in (
        (0, ds_far, ds_near, qq, SCALING, dk_own), (1, p_far, p_near, gg, 1.0, dv_own)
    ):
        shared = dot(far, rows, TN) * scale
        for j, out in enumerate((d_mine, d_other, d_ra, d_rb, d_rc)):
            out[part] = shared[j * BLOCK : (j + 1) * BLOCK].astype(BF16)
        low, high = [dot(close[halves[n]], rows[halves[n]], TN) * scale for n in range(2)]
        d_prev[part] = low[:BLOCK].astype(BF16)
        d_next[part] = high[2 * BLOCK :].astype(BF16)
        own[...] = low[BLOCK:] + high[: 2 * BLOCK]


def head_slices(ref):
    return [slice(h * HD, (h + 1) * HD) for h in range(ref.shape[-1] // HD)]


def stats_kernel(k, v, mine, other, stats):
    for h, lanes in enumerate(head_slices(k)):
        gq = jnp.concatenate([mine[0, :, lanes], other[0, :, lanes]], axis=0)
        gg = jnp.concatenate([mine[3, :, lanes], other[3, :, lanes]], axis=0)
        s = dot(k[:, lanes], gq, NT)
        top = jnp.max(s, axis=0, keepdims=True)
        e = jnp.exp2((s - top) * EXP2)
        dp = dot(v[:, lanes], gg, NT)
        stats[h, 0:1] = top * SCALING
        stats[h, 1:2] = jnp.sum(e, axis=0, keepdims=True)
        stats[h, 2:3] = jnp.sum(e * dp, axis=0, keepdims=True)


def global_kernel(k, v, mine, other, stats, dk_in, dv_in, d_mine, d_other, dk_out, dv_out):
    for h, lanes in enumerate(head_slices(k)):
        gq = jnp.concatenate([mine[0, :, lanes], other[0, :, lanes]], axis=0)
        gg = jnp.concatenate([mine[3, :, lanes], other[3, :, lanes]], axis=0)
        kk = k[:, lanes]
        vv = v[:, lanes]
        lse = stats[h, 0:1] * LOG2E
        delta = stats[h, 1:2]
        p = jnp.exp2(dot(kk, gq, NT) * EXP2 - lse)
        ph = p.astype(BF16)
        ds = (p * (dot(vv, gg, NT) - delta)).astype(BF16)
        acc = dot(ph, vv, TN).astype(BF16)
        dq = (dot(ds, kk, TN) * SCALING).astype(BF16)
        d_mine[0, :, lanes] = acc[:BLOCK]
        d_mine[1, :, lanes] = dq[:BLOCK]
        d_other[0, :, lanes] = acc[BLOCK:]
        d_other[1, :, lanes] = dq[BLOCK:]
        dk_out[:, lanes] = dk_in[:, lanes] + dot(ds, gq, NN) * SCALING
        dv_out[:, lanes] = dv_in[:, lanes] + dot(ph, gg, NN)


def pair_kernel(flags, dk_in, dv_in, above, below, ra, rb, rc, sum_kv, got_kv, dk, dv):
    for n in range(2):
        rows = slice(n * BLOCK, (n + 1) * BLOCK)
        is_root = flags[n] == 1
        edge = below if n == 0 else above
        for part, (out, first) in enumerate(((dk, dk_in), (dv, dv_in))):
            value = first[rows] + edge[part].astype(F32)
            root = sum_kv[part].astype(F32) + got_kv[part].astype(F32)
            value = value + jnp.where(is_root, root, 0.0)
            for r, back in enumerate((ra, rb, rc)):
                value = value + jnp.where(flags[2 + r] == n, back[part].astype(F32), 0.0)
            out[rows] = value.astype(BF16)


def root_kernel(flags, sum_aq, got_aq, att_in, dq_in, att, dq, rows, sems):
    del att_in, dq_in
    is_last = flags[1] == 1

    @pl.when((flags[0] == 1) | is_last)
    def _():
        rows[...] = (sum_aq[...].astype(F32) + got_aq[...].astype(F32)).astype(BF16)
        start = pl.multiple_of(jnp.where(is_last, BLOCK, 0), BLOCK)
        copies = [
            pltpu.make_async_copy(rows.at[i], out.at[pl.ds(start, BLOCK)], sems.at[i])
            for i, out in enumerate((att, dq))
        ]
        for copy in copies:
            copy.start()
        for copy in copies:
            copy.wait()


def rows_spec(first=0, group=1):
    return pl.BlockSpec((2 * BLOCK, group * HD), lambda h: (0, h + first))


def stack_spec(depth, first=0, group=1):
    return pl.BlockSpec((depth, BLOCK, group * HD), lambda h: (0, 0, h + first))


def stat_spec(count, width, first=0, group=1):
    return pl.BlockSpec((group, count, width), lambda h: (h + first, 0, 0))


def smem_spec():
    return pl.BlockSpec(memory_space=pltpu.SMEM)


def shaped(shape, dtype):
    return jax.ShapeDtypeStruct(shape, dtype)


def add_half(a, b):
    return (a.astype(F32) + b.astype(F32)).astype(BF16)


def merge(a, b):
    top = jnp.maximum(a[:, 0], b[:, 0])
    fa = jnp.exp(a[:, 0] - top)
    fb = jnp.exp(b[:, 0] - top)
    return jnp.stack(
        [top, a[:, 1] * fa + b[:, 1] * fb, a[:, 2] * fa + b[:, 2] * fb], axis=1
    )


PARTS = ((0, 2), (2, 2), (4, 2), (6, 2))
STAT_BITS = (3, 2, 4, 1, 0)


def device_body(queries, key_rows, value_rows, sink_logits, partner, block_pick, out_grad):
    q, k, v, g = queries[0], key_rows[0], value_rows[0], out_grad[0]
    tokens, width = q.shape
    heads = width // HD
    two = math.gcd(heads, 2)
    four = math.gcd(heads, 4)
    place = lax.axis_index("ctx")
    is_first = (place == 0).astype(jnp.int32)
    is_last = (place == CTX - 1).astype(jnp.int32)

    def call(kernel, ins, outs, scalars=0, grid=None, **more):
        return lambda *operands: pl.pallas_call(
            kernel,
            grid=(heads if grid is None else grid,),
            in_specs=[smem_spec()] * scalars + ins,
            out_specs=[spec for spec, _ in outs],
            out_shape=[shape for _, shape in outs],
            interpret=INTERPRET,
            **more,
        )(*operands)

    masks = partner[:, 0]
    bit_places = sum((masks >= (1 << b)).astype(jnp.int32) for b in range(1, BITS))
    partner_place = jnp.bitwise_xor(place, masks)
    ctx_match = jnp.arange(CTX)[None, :] == partner_place[:, None]
    wanted = jnp.sum(jnp.where(ctx_match, block_pick[0], 0), axis=1)

    def cut(array, block):
        return lax.dynamic_slice_in_dim(array, block * BLOCK, BLOCK, 0)

    up = [(i, i + 1) for i in range(CTX - 1)]
    down = [(i + 1, i) for i in range(CTX - 1)]
    prev = move(jnp.stack([k[tokens - BLOCK :], v[tokens - BLOCK :]]), up)
    nxt = move(jnp.stack([k[:BLOCK], v[:BLOCK]]), down)
    heads_of = jnp.stack([array[:BLOCK] for array in (q, k, v, g)])
    tails_of = jnp.stack([array[tokens - BLOCK :] for array in (q, k, v, g)])
    mine = jnp.where(place == CTX - 1, tails_of, heads_of)
    packages = [jnp.stack([cut(k, wanted[r]), cut(v, wanted[r])]) for r in range(ROUNDS)]
    fetched = []
    for step, bit in enumerate((4, 3, 2, 1)):
        got = move(mine, spread_pairs(bit))
        if step < ROUNDS:
            fetched.append(routed(packages[step], bit_places[step]))
        mask = (2 << bit) - 1
        low = place & mask
        takes = (low == (1 << bit)) | (low == mask - (1 << bit))
        mine = jnp.where(takes, got, mine)
    other = flip(mine, 0)

    (stats,) = call(
        stats_kernel,
        [rows_spec(0, four)] * 2 + [stack_spec(4, 0, four)] * 2,
        [(stat_spec(3, 2 * BLOCK, 0, four), shaped((heads, 3, 2 * BLOCK), F32))],
        0,
        heads // four,
    )(k, v, mine, other)
    for bit in STAT_BITS:
        sent = stats if bit else jnp.concatenate([stats[:, :, BLOCK:], stats[:, :, :BLOCK]], axis=2)
        arrived = flip(sent, bit)
        stats = merge(stats, arrived)
    sink_column = sink_logits[:, None]
    top = jnp.maximum(stats[:, 0], sink_column)
    factor = jnp.exp(stats[:, 0] - top)
    total = jnp.exp(sink_column - top) + stats[:, 1] * factor
    lse = top + jnp.log(total)
    delta = stats[:, 2] * factor / total
    global_sink = jnp.sum(jnp.exp(sink_column - lse) * delta, axis=1)
    lse_delta = jnp.stack([lse, delta], axis=1)

    pair = shaped((2, BLOCK, width), BF16)
    half_rows = shaped((tokens, width), BF16)
    full_rows = shaped((tokens, width), F32)
    ends = jnp.stack([is_first, is_last])
    shapes = [half_rows] * 2 + [full_rows] * 2 + [pair] * 7 + [shaped((heads, 8, HD), F32)]
    inputs = (ends, sink_logits, q, g, k, v, prev, nxt, mine, other, *fetched)
    kept = []
    parts = PARTS if heads == 8 else ((0, heads),)
    for first, count in parts:
        specs = [rows_spec(first)] * 4 + [stack_spec(2, first)] * 7 + [stat_spec(8, HD, first)]
        kept = call(
            lambda *refs, first=first: regular_kernel(*refs, first_head=first),
            [rows_spec(first)] * 4 + [stack_spec(2, first)] * 2 + [stack_spec(4, first)] * 2
            + [stack_spec(2, first)] * 3 + [pl.BlockSpec(memory_space=pl.ANY)] * len(kept),
            list(zip(specs, shapes)),
            2,
            count,
            input_output_aliases={len(inputs) + i: i for i in range(len(kept))},
        )(*inputs, *kept)
    (att_r, dq_r, dk_a, dv_a, d_prev, d_next, kv_mine, kv_other, *d_random, sink_part) = kept

    (aq_mine, aq_other, dk_b, dv_b) = call(
        global_kernel,
        [rows_spec(0, two)] * 2 + [stack_spec(4, 0, two)] * 2
        + [stat_spec(2, 2 * BLOCK, 0, two)] + [rows_spec(0, two)] * 2,
        [(stack_spec(2, 0, two), pair)] * 2 + [(rows_spec(0, two), full_rows)] * 2,
        0,
        heads // two,
        input_output_aliases={5: 2, 6: 3},
    )(k, v, mine, other, lse_delta, dk_a, dv_a)

    above = move(d_prev, down)
    below = move(d_next, up)
    sink_row = sink_part[:, 0]
    kv_got = flip(kv_other, 0)
    sink_got = flip(sink_row, 0)
    aq_got = flip(aq_other, 0)
    kv_sum = add_half(kv_mine, kv_got)
    aq_sum = add_half(aq_mine, aq_got)
    sink_row = sink_row + sink_got
    returned = []
    for step, bit in enumerate((1, 2, 3, 4)):
        kv_got = move(kv_sum, collect_pairs(bit))
        sink_got = flip(sink_row, bit)
        aq_got = move(aq_sum, collect_pairs(bit))
        if step < ROUNDS:
            returned.append(routed(d_random[step], bit_places[step]))
            kv_sum = add_half(kv_sum, kv_got)
            aq_sum = add_half(aq_sum, aq_got)
        sink_row = sink_row + sink_got
    sink_row = sink_row + global_sink[:, None]
    docs = lax.axis_size("dp")
    others = []
    for step in range(1, docs):
        others.append(lax.ppermute(sink_row, "dp", [(i, (i + step) % docs) for i in range(docs)]))
    for value in others:
        sink_row = sink_row + value
    sink_grad = -sink_row[:, 0] / math.sqrt(docs * CTX * tokens)

    flags = jnp.concatenate([ends, wanted.astype(jnp.int32)])
    key_grad, value_grad = call(
        pair_kernel,
        [rows_spec(0, two)] * 2 + [stack_spec(2, 0, two)] * 7,
        [(rows_spec(0, two), half_rows)] * 2,
        1,
        heads // two,
    )(flags, dk_b, dv_b, above, below, *returned, kv_sum, kv_got)
    whole = pl.BlockSpec((2, BLOCK, width), lambda h: (0, 0, 0))
    anywhere = pl.BlockSpec(memory_space=pl.ANY)
    attention, query_grad = call(
        root_kernel,
        [whole] * 2 + [anywhere] * 2,
        [(anywhere, half_rows)] * 2,
        1,
        1,
        input_output_aliases={3: 0, 4: 1},
        scratch_shapes=[pltpu.VMEM((2, BLOCK, width), BF16), pltpu.SemaphoreType.DMA((2,))],
    )(ends, aq_sum, aq_got, att_r, dq_r)
    return (attention[None], query_grad[None], key_grad[None], value_grad[None], sink_grad)


def solution(mesh):
    whole = P("dp", "ctx", "head")
    return jax.shard_map(
        device_body,
        mesh=mesh,
        in_specs=(whole, whole, whole, P("head"), P(), P("dp", None, None), whole),
        out_specs=(whole, whole, whole, whole, P("head")),
        check_vma=False,
    )
```

```python
import math

import jax
import jax.numpy as jnp
from jax import lax
from jax.experimental import pallas as pl
from jax.experimental.pallas import tpu as pltpu
from jax.sharding import PartitionSpec as P


HD = 128
BLOCK = 128
ROUNDS = 3
BITS = 5
CTX = 32
INTERPRET = False
F32 = jnp.float32
BF16 = jnp.bfloat16
SCALING = HD ** (-0.5)
LOG2E = math.log2(math.e)
EXP2 = SCALING * LOG2E
NT = (((1,), (1,)), ((), ()))
NN = (((1,), (0,)), ((), ()))
TN = (((0,), (0,)), ((), ()))


def dot(a, b, dims):
    return lax.dot_general(a, b, dims, preferred_element_type=F32)


def move(value, pairs):
    return lax.ppermute(value, "ctx", pairs)


def flip(value, bit):
    return move(value, [(i, i ^ (1 << bit)) for i in range(CTX)])


def spread_pairs(order, step):
    pairs = []
    for i in range(CTX):
        if all((i >> bit) & 1 == i & 1 for bit in order[step:]):
            pairs.append((i, i ^ (1 << order[step])))
    return pairs


def collect_pairs(order, step):
    pairs = []
    for i in range(CTX):
        differs = (i >> order[step]) & 1 != i & 1
        if differs and all((i >> bit) & 1 == i & 1 for bit in order[:step]):
            pairs.append((i, i ^ (1 << order[step])))
    return pairs


def routed(package, bit_place):
    return lax.switch(
        bit_place, [lambda value, bit=bit: flip(value, bit) for bit in range(BITS)], package
    )


def regular_kernel(
    flags, sink, q, g, k, v, prev, nxt, mine, other, ra, rb, rc,
    *refs, first_head,
):
    att, dq, dk_own, dv_own, d_prev, d_next, d_mine, d_other, d_ra, d_rb, d_rc, sink_out = refs[-12:]
    sink_h = sink[pl.program_id(0) + first_head] * (1.0 / SCALING)
    ends = (flags[0] == 1, flags[1] == 1)
    zero = jnp.zeros((BLOCK, HD), BF16)
    halves = (slice(0, BLOCK), slice(BLOCK, 2 * BLOCK))
    qq = q[...]
    gg = jnp.concatenate([jnp.where(ends[n], zero, g[halves[n]]) for n in range(2)], axis=0)
    k_shared = jnp.concatenate([mine[1], other[1], ra[0], rb[0], rc[0]], axis=0)
    v_shared = jnp.concatenate([mine[2], other[2], ra[1], rb[1], rc[1]], axis=0)
    k_line = jnp.concatenate([prev[0], k[...], nxt[0]], axis=0)
    v_line = jnp.concatenate([prev[1], v[...], nxt[1]], axis=0)
    near = [slice(n * BLOCK, (n + 3) * BLOCK) for n in range(2)]

    def joined(make):
        return jnp.concatenate([make(n) for n in range(2)], axis=0)

    def near_scores(n):
        s = dot(qq[halves[n]], k_line[near[n]], NT)
        parts = [s[:, j * BLOCK : (j + 1) * BLOCK] for j in range(3)]
        masked = 0 if n == 1 else 2
        parts[masked] = jnp.where(ends[1 - n], -jnp.inf, parts[masked])
        return jnp.concatenate(parts, axis=1)

    s_far = dot(qq, k_shared, NT)
    s_near = joined(near_scores)
    top = jnp.maximum(jnp.max(s_far, axis=1, keepdims=True), jnp.max(s_near, axis=1, keepdims=True))
    top = jnp.maximum(top, sink_h)
    e_far = jnp.exp2((s_far - top) * EXP2)
    e_near = jnp.exp2((s_near - top) * EXP2)
    sink_e = jnp.exp2((sink_h - top) * EXP2)
    total = sink_e + jnp.sum(e_far, axis=1, keepdims=True) + jnp.sum(e_near, axis=1, keepdims=True)
    inverse = 1.0 / total
    h_far = e_far.astype(BF16)
    h_near = e_near.astype(BF16)
    acc = dot(h_far, v_shared, NN) + joined(lambda n: dot(h_near[halves[n]], v_line[near[n]], NN))
    half = (acc * inverse).astype(BF16)
    att[...] = half
    delta = jnp.sum(gg.astype(F32) * half.astype(F32), axis=1, keepdims=True)
    sink_sum = jnp.sum(sink_e * inverse * delta, axis=0, keepdims=True)
    sink_out[0] = jnp.broadcast_to(sink_sum, (8, HD))
    p_far = e_far * inverse
    p_near = e_near * inverse
    ds_far = (p_far * (dot(gg, v_shared, NT) - delta)).astype(BF16)
    dp_near = joined(lambda n: dot(gg[halves[n]], v_line[near[n]], NT))
    ds_near = (p_near * (dp_near - delta)).astype(BF16)
    p_far = p_far.astype(BF16)
    p_near = p_near.astype(BF16)
    back = dot(ds_far, k_shared, NN) + joined(lambda n: dot(ds_near[halves[n]], k_line[near[n]], NN))
    dq[...] = (back * SCALING).astype(BF16)
    for part, far, close, rows, scale, own in (
        (0, ds_far, ds_near, qq, SCALING, dk_own), (1, p_far, p_near, gg, 1.0, dv_own)
    ):
        shared = dot(far, rows, TN) * scale
        for j, out in enumerate((d_mine, d_other, d_ra, d_rb, d_rc)):
            out[part] = shared[j * BLOCK : (j + 1) * BLOCK].astype(BF16)
        low, high = [dot(close[halves[n]], rows[halves[n]], TN) * scale for n in range(2)]
        d_prev[part] = low[:BLOCK].astype(BF16)
        d_next[part] = high[2 * BLOCK :].astype(BF16)
        own[...] = low[BLOCK:] + high[: 2 * BLOCK]


def head_slices(ref):
    return [slice(h * HD, (h + 1) * HD) for h in range(ref.shape[-1] // HD)]


def in_order(first, second, swap):
    return jnp.concatenate([jnp.where(swap, second, first), jnp.where(swap, first, second)], axis=0)


def stats_kernel(flags, k, v, mine, other, stats):
    swap = flags[2] == 1
    lanes_of = head_slices(k)
    for h, lanes in enumerate(lanes_of):
        row = pl.ds(pl.program_id(0) * len(lanes_of) + h, 1)
        gq = in_order(mine[0, :, lanes], other[0, :, lanes], swap)
        gg = in_order(mine[3, :, lanes], other[3, :, lanes], swap)
        s = dot(k[:, lanes], gq, NT)
        top = jnp.max(s, axis=0, keepdims=True)
        e = jnp.exp2((s - top) * EXP2)
        dp = dot(v[:, lanes], gg, NT)
        stats[0, row] = top * SCALING
        stats[1, row] = jnp.sum(e, axis=0, keepdims=True)
        stats[2, row] = jnp.sum(e * dp, axis=0, keepdims=True)


def global_kernel(
    flags, sink, k, v, mine, other, stats, dk_in, dv_in,
    d_mine, d_other, dk_out, dv_out, sink_out,
):
    swap = flags[2] == 1
    lanes_of = head_slices(k)
    for h, lanes in enumerate(lanes_of):
        number = pl.program_id(0) * len(lanes_of) + h
        row = pl.ds(number, 1)
        sink_h = sink[number]
        local = stats[0, row]
        top = jnp.maximum(local, sink_h)
        factor = jnp.exp(local - top)
        sink_e = jnp.exp(sink_h - top)
        total = sink_e + stats[1, row] * factor
        lse = (top + jnp.log(total)) * LOG2E
        delta = stats[2, row] * factor / total
        sink_out[h] = jnp.broadcast_to(jnp.sum(sink_e / total * delta, axis=1, keepdims=True), (8, HD))
        lse = jnp.where(swap, jnp.concatenate([lse[:, BLOCK:], lse[:, :BLOCK]], axis=1), lse)
        delta = jnp.where(swap, jnp.concatenate([delta[:, BLOCK:], delta[:, :BLOCK]], axis=1), delta)
        gq = jnp.concatenate([mine[0, :, lanes], other[0, :, lanes]], axis=0)
        gg = jnp.concatenate([mine[3, :, lanes], other[3, :, lanes]], axis=0)
        kk = k[:, lanes]
        vv = v[:, lanes]
        p = jnp.exp2(dot(kk, gq, NT) * EXP2 - lse)
        ph = p.astype(BF16)
        ds = (p * (dot(vv, gg, NT) - delta)).astype(BF16)
        acc = dot(ph, vv, TN).astype(BF16)
        dq = (dot(ds, kk, TN) * SCALING).astype(BF16)
        d_mine[0, :, lanes] = acc[:BLOCK]
        d_mine[1, :, lanes] = dq[:BLOCK]
        d_other[0, :, lanes] = acc[BLOCK:]
        d_other[1, :, lanes] = dq[BLOCK:]
        dk_out[:, lanes] = dk_in[:, lanes] + dot(ds, gq, NN) * SCALING
        dv_out[:, lanes] = dv_in[:, lanes] + dot(ph, gg, NN)


def pair_kernel(flags, dk_in, dv_in, above, below, ra, rb, rc, sum_kv, got_kv, dk, dv):
    for n in range(2):
        rows = slice(n * BLOCK, (n + 1) * BLOCK)
        is_root = flags[n] == 1
        edge = below if n == 0 else above
        for part, (out, first) in enumerate(((dk, dk_in), (dv, dv_in))):
            value = first[rows] + edge[part].astype(F32)
            root = sum_kv[part].astype(F32) + got_kv[part].astype(F32)
            value = value + jnp.where(is_root, root, 0.0)
            for r, back in enumerate((ra, rb, rc)):
                value = value + jnp.where(flags[2 + r] == n, back[part].astype(F32), 0.0)
            out[rows] = value.astype(BF16)


def root_kernel(flags, sum_aq, got_aq, att_in, dq_in, att, dq, rows, sems):
    del att_in, dq_in
    is_last = flags[1] == 1

    @pl.when((flags[0] == 1) | is_last)
    def _():
        rows[...] = (sum_aq[...].astype(F32) + got_aq[...].astype(F32)).astype(BF16)
        start = pl.multiple_of(jnp.where(is_last, BLOCK, 0), BLOCK)
        copies = [
            pltpu.make_async_copy(rows.at[i], out.at[pl.ds(start, BLOCK)], sems.at[i])
            for i, out in enumerate((att, dq))
        ]
        for copy in copies:
            copy.start()
        for copy in copies:
            copy.wait()


def rows_spec(first=0, group=1):
    return pl.BlockSpec((2 * BLOCK, group * HD), lambda h: (0, h + first))


def stack_spec(depth, first=0, group=1):
    return pl.BlockSpec((depth, BLOCK, group * HD), lambda h: (0, 0, h + first))


def stat_spec(count, width, first=0, group=1):
    return pl.BlockSpec((group, count, width), lambda h: (h + first, 0, 0))


def smem_spec():
    return pl.BlockSpec(memory_space=pltpu.SMEM)


def shaped(shape, dtype):
    return jax.ShapeDtypeStruct(shape, dtype)


def add_half(a, b):
    return (a.astype(F32) + b.astype(F32)).astype(BF16)


def merge(a, b):
    top = jnp.maximum(a[:1], b[:1])
    summed = a * jnp.exp(a[:1] - top) + b * jnp.exp(b[:1] - top)
    return jnp.where(lax.broadcasted_iota(jnp.int32, a.shape, 0) == 0, top, summed)


PARTS = ((0, 2), (2, 2), (4, 2), (6, 2))
STAT_BITS = (3, 2, 4, 1, 0)
SPREAD_ORDER = (4, 3, 2, 1)
FETCH_SLOTS = (1, 0, 2)
KV_ORDER = (1, 2, 3, 4)
AQ_ORDER = (4, 1, 2, 3)
BACK_SLOTS = (1, 2, 0)


def device_body(queries, key_rows, value_rows, sink_logits, partner, block_pick, out_grad):
    q, k, v, g = queries[0], key_rows[0], value_rows[0], out_grad[0]
    tokens, width = q.shape
    heads = width // HD
    two = math.gcd(heads, 2)
    four = math.gcd(heads, 4)
    place = lax.axis_index("ctx")
    is_first = (place == 0).astype(jnp.int32)
    is_last = (place == CTX - 1).astype(jnp.int32)

    def call(kernel, ins, outs, scalars=0, grid=None, **more):
        return lambda *operands: pl.pallas_call(
            kernel,
            grid=(heads if grid is None else grid,),
            in_specs=[smem_spec()] * scalars + ins,
            out_specs=[spec for spec, _ in outs],
            out_shape=[shape for _, shape in outs],
            interpret=INTERPRET,
            **more,
        )(*operands)

    masks = partner[:, 0]
    bit_places = sum((masks >= (1 << b)).astype(jnp.int32) for b in range(1, BITS))
    partner_place = jnp.bitwise_xor(place, masks)
    ctx_match = jnp.arange(CTX)[None, :] == partner_place[:, None]
    wanted = jnp.sum(jnp.where(ctx_match, block_pick[0], 0), axis=1)
    number = jnp.arange(ROUNDS)
    ahead = bit_places[None, :] < bit_places[:, None]
    ahead |= (bit_places[None, :] == bit_places[:, None]) & (number[None, :] < number[:, None])
    rank = jnp.sum(ahead.astype(jnp.int32), axis=1)
    chosen = (rank[None, :] == number[:, None]).astype(jnp.int32)
    bit_places = jnp.sum(chosen * bit_places[None, :], axis=1)
    wanted = jnp.sum(chosen * wanted[None, :], axis=1)

    def cut(array, block):
        return lax.dynamic_slice_in_dim(array, block * BLOCK, BLOCK, 0)

    up = [(i, i + 1) for i in range(CTX - 1)]
    down = [(i + 1, i) for i in range(CTX - 1)]
    prev = move(jnp.stack([k[tokens - BLOCK :], v[tokens - BLOCK :]]), up)
    nxt = move(jnp.stack([k[:BLOCK], v[:BLOCK]]), down)
    heads_of = jnp.stack([array[:BLOCK] for array in (q, k, v, g)])
    tails_of = jnp.stack([array[tokens - BLOCK :] for array in (q, k, v, g)])
    mine = jnp.where(place == CTX - 1, tails_of, heads_of)
    packages = [jnp.stack([cut(k, wanted[r]), cut(v, wanted[r])]) for r in range(ROUNDS)]
    fetched = [None] * ROUNDS
    for step, bit in enumerate(SPREAD_ORDER):
        got = move(mine, spread_pairs(SPREAD_ORDER, step))
        if step < ROUNDS:
            slot = FETCH_SLOTS[step]
            fetched[slot] = routed(packages[slot], bit_places[slot])
        core = place & 1
        takes = (place >> bit) & 1 != core
        for later in SPREAD_ORDER[step + 1 :]:
            takes &= (place >> later) & 1 == core
        mine = jnp.where(takes, got, mine)
    other = flip(mine, 0)

    ends = jnp.stack([is_first, is_last, place & 1])
    stats_shape = shaped((3, heads, 2 * BLOCK), F32)
    stats_spec = pl.BlockSpec((3, heads, 2 * BLOCK), lambda h: (0, 0, 0))
    (stats,) = call(
        stats_kernel,
        [rows_spec(0, four)] * 2 + [stack_spec(4, 0, four)] * 2,
        [(stats_spec, stats_shape)],
        1,
        heads // four,
    )(ends, k, v, mine, other)
    for bit in STAT_BITS:
        arrived = flip(stats, bit)
        stats = merge(stats, arrived)

    pair = shaped((2, BLOCK, width), BF16)
    half_rows = shaped((tokens, width), BF16)
    full_rows = shaped((tokens, width), F32)
    shapes = [half_rows] * 2 + [full_rows] * 2 + [pair] * 7 + [shaped((heads, 8, HD), F32)]
    inputs = (ends, sink_logits, q, g, k, v, prev, nxt, mine, other, *fetched)
    kept = []
    parts = PARTS if heads == 8 else ((0, heads),)
    for number, (first, count) in enumerate(parts):
        specs = [rows_spec(first)] * 4 + [stack_spec(2, first)] * 7 + [stat_spec(8, HD, first)]
        kept = call(
            lambda *refs, first=first: regular_kernel(*refs, first_head=first),
            [rows_spec(first)] * 4 + [stack_spec(2, first)] * 2 + [stack_spec(4, first)] * 2
            + [stack_spec(2, first)] * 3 + [pl.BlockSpec(memory_space=pl.ANY)] * len(kept),
            list(zip(specs, shapes)),
            2,
            count,
            input_output_aliases={len(inputs) + i: i for i in range(len(kept))},
        )(*inputs, *kept)
    (att_r, dq_r, dk_a, dv_a, d_prev, d_next, kv_mine, kv_other, *d_random, sink_part) = kept

    (aq_mine, aq_other, dk_b, dv_b, global_sink) = call(
        global_kernel,
        [rows_spec(0, two)] * 2 + [stack_spec(4, 0, two)] * 2 + [stats_spec]
        + [rows_spec(0, two)] * 2,
        [(stack_spec(2, 0, two), pair)] * 2 + [(rows_spec(0, two), full_rows)] * 2
        + [(stat_spec(8, HD, 0, two), shaped((heads, 8, HD), F32))],
        2,
        heads // two,
        input_output_aliases={7: 2, 8: 3},
    )(ends, sink_logits, k, v, mine, other, stats, dk_a, dv_a)

    above = move(d_prev, down)
    below = move(d_next, up)
    sink_row = sink_part
    kv_got = flip(kv_other, 0)
    sink_got = flip(sink_row, 0)
    aq_got = flip(aq_other, 0)
    kv_sum = add_half(kv_mine, kv_got)
    aq_sum = add_half(aq_mine, aq_got)
    sink_row = sink_row + sink_got
    returned = [None] * ROUNDS
    for step in range(4):
        kv_got = move(kv_sum, collect_pairs(KV_ORDER, step))
        sink_got = flip(sink_row, step + 1)
        aq_got = move(aq_sum, collect_pairs(AQ_ORDER, step))
        if step < ROUNDS:
            slot = BACK_SLOTS[step]
            returned[slot] = routed(d_random[slot], bit_places[slot])
            kv_sum = add_half(kv_sum, kv_got)
            aq_sum = add_half(aq_sum, aq_got)
        sink_row = sink_row + sink_got
    sink_row = sink_row + global_sink
    docs = lax.axis_size("dp")
    others = []
    for step in range(1, docs):
        others.append(lax.ppermute(sink_row, "dp", [(i, (i + step) % docs) for i in range(docs)]))
    for value in others:
        sink_row = sink_row + value
    sink_grad = -sink_row[:, 0, 0] / math.sqrt(docs * CTX * tokens)

    flags = jnp.concatenate([ends[:2], wanted.astype(jnp.int32)])
    key_grad, value_grad = call(
        pair_kernel,
        [rows_spec(0, two)] * 2 + [stack_spec(2, 0, two)] * 7,
        [(rows_spec(0, two), half_rows)] * 2,
        1,
        heads // two,
    )(flags, dk_b, dv_b, above, below, *returned, kv_sum, kv_got)
    whole = pl.BlockSpec((2, BLOCK, width), lambda h: (0, 0, 0))
    anywhere = pl.BlockSpec(memory_space=pl.ANY)
    attention, query_grad = call(
        root_kernel,
        [whole] * 2 + [anywhere] * 2,
        [(anywhere, half_rows)] * 2,
        1,
        1,
        input_output_aliases={3: 0, 4: 1},
        scratch_shapes=[pltpu.VMEM((2, BLOCK, width), BF16), pltpu.SemaphoreType.DMA((2,))],
    )(ends, aq_sum, aq_got, att_r, dq_r)
    return (attention[None], query_grad[None], key_grad[None], value_grad[None], sink_grad)


def solution(mesh):
    whole = P("dp", "ctx", "head")
    return jax.shard_map(
        device_body,
        mesh=mesh,
        in_specs=(whole, whole, whole, P("head"), P(), P("dp", None, None), whole),
        out_specs=(whole, whole, whole, whole, P("head")),
        check_vma=False,
    )
```

```python
import math

import jax
import jax.numpy as jnp
from jax import lax
from jax.experimental import pallas as pl
from jax.experimental.pallas import tpu as pltpu
from jax.sharding import PartitionSpec as P


HD = 128
BLOCK = 128
ROUNDS = 3
BITS = 5
CTX = 32
INTERPRET = False
F32 = jnp.float32
BF16 = jnp.bfloat16
SCALING = HD ** (-0.5)
LOG2E = math.log2(math.e)
EXP2 = SCALING * LOG2E
NT = (((1,), (1,)), ((), ()))
NN = (((1,), (0,)), ((), ()))
TN = (((0,), (0,)), ((), ()))


def dot(a, b, dims):
    return lax.dot_general(a, b, dims, preferred_element_type=F32)


def move(value, pairs):
    return lax.ppermute(value, "ctx", pairs)


def flip(value, bit):
    return move(value, [(i, i ^ (1 << bit)) for i in range(CTX)])


TREE = (
    (
        (((0, 0), (0, 2)),),
        (((0, 0), (0, 6)),),
        (((0, 0), (1, 0)),),
    ),
    (
        (((0, 0), (0, 1)), ((0, 2), (0, 4)), ((0, 6), (0, 5)), ((1, 0), (1, 1))),
        (((0, 0), (0, 7)), ((0, 2), (1, 2)), ((0, 6), (1, 6)), ((1, 0), (1, 7))),
    ),
    (
        (((0, 4), (0, 3)), ((1, 2), (1, 3)), ((1, 6), (1, 5))),
        (((0, 4), (1, 4)),),
    ),
)


def tree_pairs(edges):
    pairs = [(a[0] * 16 + a[1] * 2, b[0] * 16 + b[1] * 2) for a, b in edges]
    return pairs + [(CTX - 1 - i, CTX - 1 - j) for i, j in pairs]


def member(place, devices):
    bits = sum(1 << i for i in devices)
    return (jnp.uint32(bits) >> place.astype(jnp.uint32)) & jnp.uint32(1) == 1


def routed(package, bit_place):
    return lax.switch(
        bit_place, [lambda value, bit=bit: flip(value, bit) for bit in range(BITS)], package
    )


def regular_kernel(
    flags, sink, q, g, k, v, prev, nxt, mine, other, ra, rb, rc,
    *refs, first_head,
):
    att, dq, dk_own, dv_own, d_prev, d_next, d_mine, d_other, d_ra, d_rb, d_rc, sink_out = refs[-12:]
    sink_h = sink[pl.program_id(0) + first_head] * (1.0 / SCALING)
    ends = (flags[0] == 1, flags[1] == 1)
    zero = jnp.zeros((BLOCK, HD), BF16)
    halves = (slice(0, BLOCK), slice(BLOCK, 2 * BLOCK))
    qq = q[...]
    gg = jnp.concatenate([jnp.where(ends[n], zero, g[halves[n]]) for n in range(2)], axis=0)
    k_shared = jnp.concatenate([mine[1], other[1], ra[0], rb[0], rc[0]], axis=0)
    v_shared = jnp.concatenate([mine[2], other[2], ra[1], rb[1], rc[1]], axis=0)
    k_line = jnp.concatenate([prev[0], k[...], nxt[0]], axis=0)
    v_line = jnp.concatenate([prev[1], v[...], nxt[1]], axis=0)
    near = [slice(n * BLOCK, (n + 3) * BLOCK) for n in range(2)]

    def joined(make):
        return jnp.concatenate([make(n) for n in range(2)], axis=0)

    def near_scores(n):
        s = dot(qq[halves[n]], k_line[near[n]], NT)
        parts = [s[:, j * BLOCK : (j + 1) * BLOCK] for j in range(3)]
        masked = 0 if n == 1 else 2
        parts[masked] = jnp.where(ends[1 - n], -jnp.inf, parts[masked])
        return jnp.concatenate(parts, axis=1)

    s_far = dot(qq, k_shared, NT)
    s_near = joined(near_scores)
    top = jnp.maximum(jnp.max(s_far, axis=1, keepdims=True), jnp.max(s_near, axis=1, keepdims=True))
    top = jnp.maximum(top, sink_h)
    e_far = jnp.exp2((s_far - top) * EXP2)
    e_near = jnp.exp2((s_near - top) * EXP2)
    sink_e = jnp.exp2((sink_h - top) * EXP2)
    total = sink_e + jnp.sum(e_far, axis=1, keepdims=True) + jnp.sum(e_near, axis=1, keepdims=True)
    inverse = 1.0 / total
    h_far = e_far.astype(BF16)
    h_near = e_near.astype(BF16)
    acc = dot(h_far, v_shared, NN) + joined(lambda n: dot(h_near[halves[n]], v_line[near[n]], NN))
    half = (acc * inverse).astype(BF16)
    att[...] = half
    delta = jnp.sum(gg.astype(F32) * half.astype(F32), axis=1, keepdims=True)
    sink_sum = jnp.sum(sink_e * inverse * delta, axis=0, keepdims=True)
    sink_out[0] = jnp.broadcast_to(sink_sum, (8, HD))
    p_far = e_far * inverse
    p_near = e_near * inverse
    ds_far = (p_far * (dot(gg, v_shared, NT) - delta)).astype(BF16)
    dp_near = joined(lambda n: dot(gg[halves[n]], v_line[near[n]], NT))
    ds_near = (p_near * (dp_near - delta)).astype(BF16)
    p_far = p_far.astype(BF16)
    p_near = p_near.astype(BF16)
    back = dot(ds_far, k_shared, NN) + joined(lambda n: dot(ds_near[halves[n]], k_line[near[n]], NN))
    dq[...] = (back * SCALING).astype(BF16)
    for part, far, close, rows, scale, own in (
        (0, ds_far, ds_near, qq, SCALING, dk_own), (1, p_far, p_near, gg, 1.0, dv_own)
    ):
        shared = dot(far, rows, TN) * scale
        for j, out in enumerate((d_mine, d_other, d_ra, d_rb, d_rc)):
            out[part] = shared[j * BLOCK : (j + 1) * BLOCK].astype(BF16)
        low, high = [dot(close[halves[n]], rows[halves[n]], TN) * scale for n in range(2)]
        d_prev[part] = low[:BLOCK].astype(BF16)
        d_next[part] = high[2 * BLOCK :].astype(BF16)
        own[...] = low[BLOCK:] + high[: 2 * BLOCK]


def head_slices(ref):
    return [slice(h * HD, (h + 1) * HD) for h in range(ref.shape[-1] // HD)]


def in_order(first, second, swap):
    return jnp.concatenate([jnp.where(swap, second, first), jnp.where(swap, first, second)], axis=0)


def stats_kernel(flags, k, v, mine, other, stats):
    swap = flags[2] == 1
    lanes_of = head_slices(k)
    for h, lanes in enumerate(lanes_of):
        row = pl.ds(pl.program_id(0) * len(lanes_of) + h, 1)
        gq = in_order(mine[0, :, lanes], other[0, :, lanes], swap)
        gg = in_order(mine[3, :, lanes], other[3, :, lanes], swap)
        s = dot(k[:, lanes], gq, NT)
        top = jnp.max(s, axis=0, keepdims=True)
        e = jnp.exp2((s - top) * EXP2)
        dp = dot(v[:, lanes], gg, NT)
        stats[0, row] = top * SCALING
        stats[1, row] = jnp.sum(e, axis=0, keepdims=True)
        stats[2, row] = jnp.sum(e * dp, axis=0, keepdims=True)


def global_kernel(
    flags, sink, k, v, mine, other, stats, dk_in, dv_in,
    d_mine, d_other, dk_out, dv_out, sink_out,
):
    swap = flags[2] == 1
    lanes_of = head_slices(k)
    for h, lanes in enumerate(lanes_of):
        number = pl.program_id(0) * len(lanes_of) + h
        row = pl.ds(number, 1)
        sink_h = sink[number]
        local = stats[0, row]
        top = jnp.maximum(local, sink_h)
        factor = jnp.exp(local - top)
        sink_e = jnp.exp(sink_h - top)
        total = sink_e + stats[1, row] * factor
        lse = (top + jnp.log(total)) * LOG2E
        delta = stats[2, row] * factor / total
        sink_out[h] = jnp.broadcast_to(jnp.sum(sink_e / total * delta, axis=1, keepdims=True), (8, HD))
        lse = jnp.where(swap, jnp.concatenate([lse[:, BLOCK:], lse[:, :BLOCK]], axis=1), lse)
        delta = jnp.where(swap, jnp.concatenate([delta[:, BLOCK:], delta[:, :BLOCK]], axis=1), delta)
        gq = jnp.concatenate([mine[0, :, lanes], other[0, :, lanes]], axis=0)
        gg = jnp.concatenate([mine[3, :, lanes], other[3, :, lanes]], axis=0)
        kk = k[:, lanes]
        vv = v[:, lanes]
        p = jnp.exp2(dot(kk, gq, NT) * EXP2 - lse)
        ph = p.astype(BF16)
        ds = (p * (dot(vv, gg, NT) - delta)).astype(BF16)
        acc = dot(ph, vv, TN).astype(BF16)
        dq = (dot(ds, kk, TN) * SCALING).astype(BF16)
        d_mine[0, :, lanes] = acc[:BLOCK]
        d_mine[1, :, lanes] = dq[:BLOCK]
        d_other[0, :, lanes] = acc[BLOCK:]
        d_other[1, :, lanes] = dq[BLOCK:]
        dk_out[:, lanes] = dk_in[:, lanes] + dot(ds, gq, NN) * SCALING
        dv_out[:, lanes] = dv_in[:, lanes] + dot(ph, gg, NN)


def pair_kernel(flags, dk_in, dv_in, above, below, ra, rb, rc, own, ga, gb, gc, dk, dv):
    for n in range(2):
        rows = slice(n * BLOCK, (n + 1) * BLOCK)
        is_root = flags[n] == 1
        edge = below if n == 0 else above
        for part, (out, first) in enumerate(((dk, dk_in), (dv, dv_in))):
            value = first[rows] + edge[part].astype(F32)
            root = sum(ref[0, part].astype(F32) for ref in (own, ga, gb, gc))
            value = value + jnp.where(is_root, root, 0.0)
            for r, back in enumerate((ra, rb, rc)):
                value = value + jnp.where(flags[2 + r] == n, back[part].astype(F32), 0.0)
            out[rows] = value.astype(BF16)


def root_kernel(flags, own, ga, gb, gc, att_in, dq_in, att, dq, rows, sems):
    del att_in, dq_in
    is_last = flags[1] == 1

    @pl.when((flags[0] == 1) | is_last)
    def _():
        rows[...] = sum(ref[0].astype(F32) for ref in (own, ga, gb, gc)).astype(BF16)
        start = pl.multiple_of(jnp.where(is_last, BLOCK, 0), BLOCK)
        copies = [
            pltpu.make_async_copy(rows.at[i], out.at[pl.ds(start, BLOCK)], sems.at[i])
            for i, out in enumerate((att, dq))
        ]
        for copy in copies:
            copy.start()
        for copy in copies:
            copy.wait()


def rows_spec(first=0, group=1):
    return pl.BlockSpec((2 * BLOCK, group * HD), lambda h: (0, h + first))


def stack_spec(depth, first=0, group=1):
    return pl.BlockSpec((depth, BLOCK, group * HD), lambda h: (0, 0, h + first))


def stat_spec(count, width, first=0, group=1):
    return pl.BlockSpec((group, count, width), lambda h: (h + first, 0, 0))


def smem_spec():
    return pl.BlockSpec(memory_space=pltpu.SMEM)


def shaped(shape, dtype):
    return jax.ShapeDtypeStruct(shape, dtype)


def add_half(a, b):
    return (a.astype(F32) + b.astype(F32)).astype(BF16)


def merge(a, b):
    top = jnp.maximum(a[:1], b[:1])
    summed = a * jnp.exp(a[:1] - top) + b * jnp.exp(b[:1] - top)
    return jnp.where(lax.broadcasted_iota(jnp.int32, a.shape, 0) == 0, top, summed)


PARTS = ((0, 2), (2, 2), (4, 2), (6, 2))
STAT_BITS = (3, 2, 4, 1, 0)
FETCH_SLOTS = (1, 0, 2)
BACK_SLOTS = (2, 0, 1)


def device_body(queries, key_rows, value_rows, sink_logits, partner, block_pick, out_grad):
    q, k, v, g = queries[0], key_rows[0], value_rows[0], out_grad[0]
    tokens, width = q.shape
    heads = width // HD
    two = math.gcd(heads, 2)
    four = math.gcd(heads, 4)
    place = lax.axis_index("ctx")
    is_first = (place == 0).astype(jnp.int32)
    is_last = (place == CTX - 1).astype(jnp.int32)

    def call(kernel, ins, outs, scalars=0, grid=None, **more):
        return lambda *operands: pl.pallas_call(
            kernel,
            grid=(heads if grid is None else grid,),
            in_specs=[smem_spec()] * scalars + ins,
            out_specs=[spec for spec, _ in outs],
            out_shape=[shape for _, shape in outs],
            interpret=INTERPRET,
            **more,
        )(*operands)

    heads_of = jnp.stack([array[:BLOCK] for array in (q, k, v, g)])
    tails_of = jnp.stack([array[tokens - BLOCK :] for array in (q, k, v, g)])
    mine = jnp.where(place == CTX - 1, tails_of, heads_of)
    mine, partner, block_pick = lax.optimization_barrier((mine, partner, block_pick))
    masks = partner[:, 0]
    bit_places = sum((masks >= (1 << b)).astype(jnp.int32) for b in range(1, BITS))
    partner_place = jnp.bitwise_xor(place, masks)
    ctx_match = jnp.arange(CTX)[None, :] == partner_place[:, None]
    wanted = jnp.sum(jnp.where(ctx_match, block_pick[0], 0), axis=1)
    number = jnp.arange(ROUNDS)
    ahead = bit_places[None, :] < bit_places[:, None]
    ahead |= (bit_places[None, :] == bit_places[:, None]) & (number[None, :] < number[:, None])
    rank = jnp.sum(ahead.astype(jnp.int32), axis=1)
    chosen = (rank[None, :] == number[:, None]).astype(jnp.int32)
    bit_places = jnp.sum(chosen * bit_places[None, :], axis=1)
    wanted = jnp.sum(chosen * wanted[None, :], axis=1)

    def cut(array, block):
        return lax.dynamic_slice_in_dim(array, block * BLOCK, BLOCK, 0)

    up = [(i, i + 1) for i in range(CTX - 1)]
    down = [(i + 1, i) for i in range(CTX - 1)]
    prev = move(jnp.stack([k[tokens - BLOCK :], v[tokens - BLOCK :]]), up)
    nxt = move(jnp.stack([k[:BLOCK], v[:BLOCK]]), down)
    packages = [jnp.stack([cut(k, wanted[r]), cut(v, wanted[r])]) for r in range(ROUNDS)]
    fetched = [None] * ROUNDS
    for step, stage in enumerate(TREE):
        gots = [move(mine, tree_pairs(edges)) for edges in stage]
        slot = FETCH_SLOTS[step]
        fetched[slot] = routed(packages[slot], bit_places[slot])
        for edges, got in zip(stage, gots):
            mine = jnp.where(member(place, [j for _, j in tree_pairs(edges)]), got, mine)
    other = flip(mine, 0)

    ends = jnp.stack([is_first, is_last, place & 1])
    stats_shape = shaped((3, heads, 2 * BLOCK), F32)
    stats_spec = pl.BlockSpec((3, heads, 2 * BLOCK), lambda h: (0, 0, 0))
    (stats,) = call(
        stats_kernel,
        [rows_spec(0, four)] * 2 + [stack_spec(4, 0, four)] * 2,
        [(stats_spec, stats_shape)],
        1,
        heads // four,
    )(ends, k, v, mine, other)
    for bit in STAT_BITS:
        arrived = flip(stats, bit)
        stats = merge(stats, arrived)

    pair = shaped((2, BLOCK, width), BF16)
    half_rows = shaped((tokens, width), BF16)
    full_rows = shaped((tokens, width), F32)
    shapes = [half_rows] * 2 + [full_rows] * 2 + [pair] * 7 + [shaped((heads, 8, HD), F32)]
    inputs = (ends, sink_logits, q, g, k, v, prev, nxt, mine, other, *fetched)
    kept = []
    parts = PARTS if heads == 8 else ((0, heads),)
    for number, (first, count) in enumerate(parts):
        specs = [rows_spec(first)] * 4 + [stack_spec(2, first)] * 7 + [stat_spec(8, HD, first)]
        kept = call(
            lambda *refs, first=first: regular_kernel(*refs, first_head=first),
            [rows_spec(first)] * 4 + [stack_spec(2, first)] * 2 + [stack_spec(4, first)] * 2
            + [stack_spec(2, first)] * 3 + [pl.BlockSpec(memory_space=pl.ANY)] * len(kept),
            list(zip(specs, shapes)),
            2,
            count,
            input_output_aliases={len(inputs) + i: i for i in range(len(kept))},
        )(*inputs, *kept)
    (att_r, dq_r, dk_a, dv_a, d_prev, d_next, kv_mine, kv_other, *d_random, sink_part) = kept

    (aq_mine, aq_other, dk_b, dv_b, global_sink) = call(
        global_kernel,
        [rows_spec(0, two)] * 2 + [stack_spec(4, 0, two)] * 2 + [stats_spec]
        + [rows_spec(0, two)] * 2,
        [(stack_spec(2, 0, two), pair)] * 2 + [(rows_spec(0, two), full_rows)] * 2
        + [(stat_spec(8, HD, 0, two), shaped((heads, 8, HD), F32))],
        2,
        heads // two,
        input_output_aliases={7: 2, 8: 3},
    )(ends, sink_logits, k, v, mine, other, stats, dk_a, dv_a)

    above = move(d_prev, down)
    below = move(d_next, up)
    sink_row = sink_part
    kv_got = flip(kv_other, 0)
    sink_row = sink_row + flip(sink_row, 0)
    sink_row = sink_row + flip(sink_row, 1)
    aq_got = flip(aq_other, 0)
    joint = jnp.stack([add_half(kv_mine, kv_got), add_half(aq_mine, aq_got)])
    returned = [None] * ROUNDS
    for step, stage in enumerate(TREE[::-1]):
        gots = [move(joint, [(j, i) for i, j in tree_pairs(edges)]) for edges in stage]
        sink_got = flip(sink_row, step + 2)
        slot = BACK_SLOTS[step]
        returned[slot] = routed(d_random[slot], bit_places[slot])
        sink_row = sink_row + sink_got
        if step < 2:
            joint = (joint.astype(F32) + sum(got.astype(F32) for got in gots)).astype(BF16)
    sink_row = sink_row + global_sink
    docs = lax.axis_size("dp")
    others = []
    for step in range(1, docs):
        others.append(lax.ppermute(sink_row, "dp", [(i, (i + step) % docs) for i in range(docs)]))
    for value in others:
        sink_row = sink_row + value
    sink_grad = -sink_row[:, 0, 0] / math.sqrt(docs * CTX * tokens)

    flags = jnp.concatenate([ends[:2], wanted.astype(jnp.int32)])
    key_grad, value_grad = call(
        pair_kernel,
        [rows_spec(0, two)] * 2 + [stack_spec(2, 0, two)] * 5
        + [pl.BlockSpec((1, 2, BLOCK, two * HD), lambda h: (0, 0, 0, h))] * 4,
        [(rows_spec(0, two), half_rows)] * 2,
        1,
        heads // two,
    )(flags, dk_b, dv_b, above, below, *returned, joint, *gots)
    whole = pl.BlockSpec((1, 2, BLOCK, width), lambda h: (1, 0, 0, 0))
    anywhere = pl.BlockSpec(memory_space=pl.ANY)
    attention, query_grad = call(
        root_kernel,
        [whole] * 4 + [anywhere] * 2,
        [(anywhere, half_rows)] * 2,
        1,
        1,
        input_output_aliases={5: 0, 6: 1},
        scratch_shapes=[pltpu.VMEM((2, BLOCK, width), BF16), pltpu.SemaphoreType.DMA((2,))],
    )(ends, joint, *gots, att_r, dq_r)
    return (attention[None], query_grad[None], key_grad[None], value_grad[None], sink_grad)


def solution(mesh):
    whole = P("dp", "ctx", "head")
    return jax.shard_map(
        device_body,
        mesh=mesh,
        in_specs=(whole, whole, whole, P("head"), P(), P("dp", None, None), whole),
        out_specs=(whole, whole, whole, whole, P("head")),
        check_vma=False,
    )
```

```python
import math

import jax
import jax.numpy as jnp
from jax import lax
from jax.experimental import pallas as pl
from jax.experimental.pallas import tpu as pltpu
from jax.sharding import PartitionSpec as P


HD = 128
BLOCK = 128
ROUNDS = 3
BITS = 5
CTX = 32
INTERPRET = False
F32 = jnp.float32
BF16 = jnp.bfloat16
SCALING = HD ** (-0.5)
LOG2E = math.log2(math.e)
EXP2 = SCALING * LOG2E
NT = (((1,), (1,)), ((), ()))
NN = (((1,), (0,)), ((), ()))
TN = (((0,), (0,)), ((), ()))


def dot(a, b, dims):
    return lax.dot_general(a, b, dims, preferred_element_type=F32)


def move(value, pairs):
    return lax.ppermute(value, "ctx", pairs)


def flip(value, bit):
    return move(value, [(i, i ^ (1 << bit)) for i in range(CTX)])


TREE = (
    (
        (((0, 0), (0, 3)),),
        (((0, 0), (0, 5)),),
    ),
    (
        (((0, 0), (0, 7)), ((0, 3), (0, 4)), ((0, 5), (0, 6))),
        (((0, 0), (1, 0)), ((0, 3), (1, 3)), ((0, 5), (1, 5))),
    ),
    (
        (
            ((0, 0), (0, 1)), ((0, 3), (0, 2)), ((1, 0), (1, 1)), ((1, 3), (1, 2)),
            ((0, 4), (1, 4)), ((0, 6), (1, 6)), ((0, 7), (1, 7)),
        ),
    ),
)


def tree_pairs(edges):
    pairs = [(a[0] * 16 + a[1] * 2, b[0] * 16 + b[1] * 2) for a, b in edges]
    return pairs + [(CTX - 1 - i, CTX - 1 - j) for i, j in pairs]


def member(place, devices):
    bits = sum(1 << i for i in devices)
    return (jnp.uint32(bits) >> place.astype(jnp.uint32)) & jnp.uint32(1) == 1


def routed(package, bit_place):
    return lax.switch(
        bit_place, [lambda value, bit=bit: flip(value, bit) for bit in range(BITS)], package
    )


def regular_kernel(
    flags, sink, q, g, k, v, prev, nxt, mine, other, ra, rb, rc,
    *refs, first_head,
):
    att, dq, dk_own, dv_own, d_prev, d_next, d_mine, d_other, d_ra, d_rb, d_rc, sink_out = refs[-12:]
    sink_h = sink[pl.program_id(0) + first_head] * (1.0 / SCALING)
    ends = (flags[0] == 1, flags[1] == 1)
    zero = jnp.zeros((BLOCK, HD), BF16)
    halves = (slice(0, BLOCK), slice(BLOCK, 2 * BLOCK))
    qq = q[...]
    gg = jnp.concatenate([jnp.where(ends[n], zero, g[halves[n]]) for n in range(2)], axis=0)
    k_shared = jnp.concatenate([mine[1], other[1], ra[0], rb[0], rc[0]], axis=0)
    v_shared = jnp.concatenate([mine[2], other[2], ra[1], rb[1], rc[1]], axis=0)
    k_line = jnp.concatenate([prev[0], k[...], nxt[0]], axis=0)
    v_line = jnp.concatenate([prev[1], v[...], nxt[1]], axis=0)
    near = [slice(n * BLOCK, (n + 3) * BLOCK) for n in range(2)]

    def joined(make):
        return jnp.concatenate([make(n) for n in range(2)], axis=0)

    def near_scores(n):
        s = dot(qq[halves[n]], k_line[near[n]], NT)
        parts = [s[:, j * BLOCK : (j + 1) * BLOCK] for j in range(3)]
        masked = 0 if n == 1 else 2
        parts[masked] = jnp.where(ends[1 - n], -jnp.inf, parts[masked])
        return jnp.concatenate(parts, axis=1)

    s_far = dot(qq, k_shared, NT)
    s_near = joined(near_scores)
    top = jnp.maximum(jnp.max(s_far, axis=1, keepdims=True), jnp.max(s_near, axis=1, keepdims=True))
    top = jnp.maximum(top, sink_h)
    e_far = jnp.exp2((s_far - top) * EXP2)
    e_near = jnp.exp2((s_near - top) * EXP2)
    sink_e = jnp.exp2((sink_h - top) * EXP2)
    total = sink_e + jnp.sum(e_far, axis=1, keepdims=True) + jnp.sum(e_near, axis=1, keepdims=True)
    inverse = 1.0 / total
    h_far = e_far.astype(BF16)
    h_near = e_near.astype(BF16)
    acc = dot(h_far, v_shared, NN) + joined(lambda n: dot(h_near[halves[n]], v_line[near[n]], NN))
    half = (acc * inverse).astype(BF16)
    att[...] = half
    delta = jnp.sum(gg.astype(F32) * half.astype(F32), axis=1, keepdims=True)
    sink_sum = jnp.sum(sink_e * inverse * delta, axis=0, keepdims=True)
    sink_out[0] = jnp.broadcast_to(sink_sum, (8, HD))
    p_far = e_far * inverse
    p_near = e_near * inverse
    ds_far = (p_far * (dot(gg, v_shared, NT) - delta)).astype(BF16)
    dp_near = joined(lambda n: dot(gg[halves[n]], v_line[near[n]], NT))
    ds_near = (p_near * (dp_near - delta)).astype(BF16)
    p_far = p_far.astype(BF16)
    p_near = p_near.astype(BF16)
    back = dot(ds_far, k_shared, NN) + joined(lambda n: dot(ds_near[halves[n]], k_line[near[n]], NN))
    dq[...] = (back * SCALING).astype(BF16)
    for part, far, close, rows, scale, own in (
        (0, ds_far, ds_near, qq, SCALING, dk_own), (1, p_far, p_near, gg, 1.0, dv_own)
    ):
        shared = dot(far, rows, TN) * scale
        for j, out in enumerate((d_mine, d_other, d_ra, d_rb, d_rc)):
            out[part] = shared[j * BLOCK : (j + 1) * BLOCK].astype(BF16)
        low, high = [dot(close[halves[n]], rows[halves[n]], TN) * scale for n in range(2)]
        d_prev[part] = low[:BLOCK].astype(BF16)
        d_next[part] = high[2 * BLOCK :].astype(BF16)
        own[...] = low[BLOCK:] + high[: 2 * BLOCK]


def head_slices(ref):
    return [slice(h * HD, (h + 1) * HD) for h in range(ref.shape[-1] // HD)]


def in_order(first, second, swap):
    return jnp.concatenate([jnp.where(swap, second, first), jnp.where(swap, first, second)], axis=0)


def stats_kernel(flags, k, v, mine, other, stats):
    swap = flags[2] == 1
    lanes_of = head_slices(k)
    for h, lanes in enumerate(lanes_of):
        row = pl.ds(pl.program_id(0) * len(lanes_of) + h, 1)
        gq = in_order(mine[0, :, lanes], other[0, :, lanes], swap)
        gg = in_order(mine[3, :, lanes], other[3, :, lanes], swap)
        s = dot(k[:, lanes], gq, NT)
        top = jnp.max(s, axis=0, keepdims=True)
        e = jnp.exp2((s - top) * EXP2)
        dp = dot(v[:, lanes], gg, NT)
        stats[0, row] = top * SCALING
        stats[1, row] = jnp.sum(e, axis=0, keepdims=True)
        stats[2, row] = jnp.sum(e * dp, axis=0, keepdims=True)


def global_kernel(
    flags, sink, k, v, mine, other, stats, dk_in, dv_in,
    d_mine, d_other, dk_out, dv_out, sink_out,
):
    swap = flags[2] == 1
    lanes_of = head_slices(k)
    for h, lanes in enumerate(lanes_of):
        number = pl.program_id(0) * len(lanes_of) + h
        row = pl.ds(number, 1)
        sink_h = sink[number]
        local = stats[0, row]
        top = jnp.maximum(local, sink_h)
        factor = jnp.exp(local - top)
        sink_e = jnp.exp(sink_h - top)
        total = sink_e + stats[1, row] * factor
        lse = (top + jnp.log(total)) * LOG2E
        delta = stats[2, row] * factor / total
        sink_out[h] = jnp.broadcast_to(jnp.sum(sink_e / total * delta, axis=1, keepdims=True), (8, HD))
        lse = jnp.where(swap, jnp.concatenate([lse[:, BLOCK:], lse[:, :BLOCK]], axis=1), lse)
        delta = jnp.where(swap, jnp.concatenate([delta[:, BLOCK:], delta[:, :BLOCK]], axis=1), delta)
        gq = jnp.concatenate([mine[0, :, lanes], other[0, :, lanes]], axis=0)
        gg = jnp.concatenate([mine[3, :, lanes], other[3, :, lanes]], axis=0)
        kk = k[:, lanes]
        vv = v[:, lanes]
        p = jnp.exp2(dot(kk, gq, NT) * EXP2 - lse)
        ph = p.astype(BF16)
        ds = (p * (dot(vv, gg, NT) - delta)).astype(BF16)
        acc = dot(ph, vv, TN).astype(BF16)
        dq = (dot(ds, kk, TN) * SCALING).astype(BF16)
        d_mine[0, :, lanes] = acc[:BLOCK]
        d_mine[1, :, lanes] = dq[:BLOCK]
        d_other[0, :, lanes] = acc[BLOCK:]
        d_other[1, :, lanes] = dq[BLOCK:]
        dk_out[:, lanes] = dk_in[:, lanes] + dot(ds, gq, NN) * SCALING
        dv_out[:, lanes] = dv_in[:, lanes] + dot(ph, gg, NN)


def pair_kernel(flags, dk_in, dv_in, above, below, ra, rb, rc, own, ga, gb, dk, dv):
    for n in range(2):
        rows = slice(n * BLOCK, (n + 1) * BLOCK)
        is_root = flags[n] == 1
        edge = below if n == 0 else above
        for part, (out, first) in enumerate(((dk, dk_in), (dv, dv_in))):
            value = first[rows] + edge[part].astype(F32)
            root = sum(ref[0, part].astype(F32) for ref in (own, ga, gb))
            value = value + jnp.where(is_root, root, 0.0)
            for r, back in enumerate((ra, rb, rc)):
                value = value + jnp.where(flags[2 + r] == n, back[part].astype(F32), 0.0)
            out[rows] = value.astype(BF16)


def root_kernel(flags, own, ga, gb, att_in, dq_in, att, dq, rows, sems):
    del att_in, dq_in
    is_last = flags[1] == 1

    @pl.when((flags[0] == 1) | is_last)
    def _():
        rows[...] = sum(ref[0].astype(F32) for ref in (own, ga, gb)).astype(BF16)
        start = pl.multiple_of(jnp.where(is_last, BLOCK, 0), BLOCK)
        copies = [
            pltpu.make_async_copy(rows.at[i], out.at[pl.ds(start, BLOCK)], sems.at[i])
            for i, out in enumerate((att, dq))
        ]
        for copy in copies:
            copy.start()
        for copy in copies:
            copy.wait()


def rows_spec(first=0, group=1):
    return pl.BlockSpec((2 * BLOCK, group * HD), lambda h: (0, h + first))


def stack_spec(depth, first=0, group=1):
    return pl.BlockSpec((depth, BLOCK, group * HD), lambda h: (0, 0, h + first))


def stat_spec(count, width, first=0, group=1):
    return pl.BlockSpec((group, count, width), lambda h: (h + first, 0, 0))


def smem_spec():
    return pl.BlockSpec(memory_space=pltpu.SMEM)


def shaped(shape, dtype):
    return jax.ShapeDtypeStruct(shape, dtype)


def add_half(a, b):
    return (a.astype(F32) + b.astype(F32)).astype(BF16)


def merge(a, b):
    top = jnp.maximum(a[:1], b[:1])
    summed = a * jnp.exp(a[:1] - top) + b * jnp.exp(b[:1] - top)
    return jnp.where(lax.broadcasted_iota(jnp.int32, a.shape, 0) == 0, top, summed)


PARTS = ((0, 2), (2, 2), (4, 2), (6, 2))
STAT_BITS = (3, 2, 4, 1, 0)
FETCH_SLOTS = (1, 0, 2)
BACK_SLOTS = (2, 0, 1)


def device_body(queries, key_rows, value_rows, sink_logits, partner, block_pick, out_grad):
    q, k, v, g = queries[0], key_rows[0], value_rows[0], out_grad[0]
    tokens, width = q.shape
    heads = width // HD
    two = math.gcd(heads, 2)
    four = math.gcd(heads, 4)
    place = lax.axis_index("ctx")
    is_first = (place == 0).astype(jnp.int32)
    is_last = (place == CTX - 1).astype(jnp.int32)

    def call(kernel, ins, outs, scalars=0, grid=None, **more):
        return lambda *operands: pl.pallas_call(
            kernel,
            grid=(heads if grid is None else grid,),
            in_specs=[smem_spec()] * scalars + ins,
            out_specs=[spec for spec, _ in outs],
            out_shape=[shape for _, shape in outs],
            interpret=INTERPRET,
            **more,
        )(*operands)

    heads_of = jnp.stack([array[:BLOCK] for array in (q, k, v, g)])
    tails_of = jnp.stack([array[tokens - BLOCK :] for array in (q, k, v, g)])
    mine = jnp.where(place == CTX - 1, tails_of, heads_of)
    mine, partner, block_pick = lax.optimization_barrier((mine, partner, block_pick))
    masks = partner[:, 0]
    bit_places = sum((masks >= (1 << b)).astype(jnp.int32) for b in range(1, BITS))
    partner_place = jnp.bitwise_xor(place, masks)
    ctx_match = jnp.arange(CTX)[None, :] == partner_place[:, None]
    wanted = jnp.sum(jnp.where(ctx_match, block_pick[0], 0), axis=1)
    number = jnp.arange(ROUNDS)
    ahead = bit_places[None, :] < bit_places[:, None]
    ahead |= (bit_places[None, :] == bit_places[:, None]) & (number[None, :] < number[:, None])
    rank = jnp.sum(ahead.astype(jnp.int32), axis=1)
    chosen = (rank[None, :] == number[:, None]).astype(jnp.int32)
    bit_places = jnp.sum(chosen * bit_places[None, :], axis=1)
    wanted = jnp.sum(chosen * wanted[None, :], axis=1)

    up = [(i, i + 1) for i in range(CTX - 1)]
    down = [(i + 1, i) for i in range(CTX - 1)]
    low_pair = jnp.stack([k[:BLOCK], v[:BLOCK]])
    high_pair = jnp.stack([k[tokens - BLOCK :], v[tokens - BLOCK :]])
    prev = move(high_pair, up)
    nxt = move(low_pair, down)
    packages = [jnp.where(wanted[r] == 0, low_pair, high_pair) for r in range(ROUNDS)]
    fetched = [None] * ROUNDS
    for step, stage in enumerate(TREE):
        gots = [move(mine, tree_pairs(edges)) for edges in stage]
        slot = FETCH_SLOTS[step]
        fetched[slot] = routed(packages[slot], bit_places[slot])
        for edges, got in zip(stage, gots):
            mine = jnp.where(member(place, [j for _, j in tree_pairs(edges)]), got, mine)
    other = flip(mine, 0)

    ends = jnp.stack([is_first, is_last, place & 1])
    stats_shape = shaped((3, heads, 2 * BLOCK), F32)
    stats_spec = pl.BlockSpec((3, heads, 2 * BLOCK), lambda h: (0, 0, 0))
    (stats,) = call(
        stats_kernel,
        [rows_spec(0, four)] * 2 + [stack_spec(4, 0, four)] * 2,
        [(stats_spec, stats_shape)],
        1,
        heads // four,
    )(ends, k, v, mine, other)
    for bit in STAT_BITS:
        arrived = flip(stats, bit)
        stats = merge(stats, arrived)

    pair = shaped((2, BLOCK, width), BF16)
    half_rows = shaped((tokens, width), BF16)
    full_rows = shaped((tokens, width), F32)
    shapes = [half_rows] * 2 + [full_rows] * 2 + [pair] * 7 + [shaped((heads, 8, HD), F32)]
    inputs = (ends, sink_logits, q, g, k, v, prev, nxt, mine, other, *fetched)
    kept = []
    parts = PARTS if heads == 8 else ((0, heads),)
    for number, (first, count) in enumerate(parts):
        specs = [rows_spec(first)] * 4 + [stack_spec(2, first)] * 7 + [stat_spec(8, HD, first)]
        kept = call(
            lambda *refs, first=first: regular_kernel(*refs, first_head=first),
            [rows_spec(first)] * 4 + [stack_spec(2, first)] * 2 + [stack_spec(4, first)] * 2
            + [stack_spec(2, first)] * 3 + [pl.BlockSpec(memory_space=pl.ANY)] * len(kept),
            list(zip(specs, shapes)),
            2,
            count,
            input_output_aliases={len(inputs) + i: i for i in range(len(kept))},
        )(*inputs, *kept)
    (att_r, dq_r, dk_a, dv_a, d_prev, d_next, kv_mine, kv_other, *d_random, sink_part) = kept

    (aq_mine, aq_other, dk_b, dv_b, global_sink) = call(
        global_kernel,
        [rows_spec(0, two)] * 2 + [stack_spec(4, 0, two)] * 2 + [stats_spec]
        + [rows_spec(0, two)] * 2,
        [(stack_spec(2, 0, two), pair)] * 2 + [(rows_spec(0, two), full_rows)] * 2
        + [(stat_spec(8, HD, 0, two), shaped((heads, 8, HD), F32))],
        2,
        heads // two,
        input_output_aliases={7: 2, 8: 3},
    )(ends, sink_logits, k, v, mine, other, stats, dk_a, dv_a)

    above = move(d_prev, down)
    below = move(d_next, up)
    sink_row = sink_part
    kv_got = flip(kv_other, 0)
    sink_row = sink_row + flip(sink_row, 0)
    sink_row = sink_row + flip(sink_row, 1)
    aq_got = flip(aq_other, 0)
    joint = jnp.stack([add_half(kv_mine, kv_got), add_half(aq_mine, aq_got)])
    returned = [None] * ROUNDS
    for step, stage in enumerate(TREE[::-1]):
        gots = [move(joint, [(j, i) for i, j in tree_pairs(edges)]) for edges in stage]
        sink_got = flip(sink_row, step + 2)
        slot = BACK_SLOTS[step]
        returned[slot] = routed(d_random[slot], bit_places[slot])
        sink_row = sink_row + sink_got
        if step < 2:
            joint = (joint.astype(F32) + sum(got.astype(F32) for got in gots)).astype(BF16)
    sink_row = sink_row + global_sink
    docs = lax.axis_size("dp")
    others = []
    for step in range(1, docs):
        others.append(lax.ppermute(sink_row, "dp", [(i, (i + step) % docs) for i in range(docs)]))
    for value in others:
        sink_row = sink_row + value
    sink_grad = -sink_row[:, 0, 0] / math.sqrt(docs * CTX * tokens)

    flags = jnp.concatenate([ends[:2], wanted.astype(jnp.int32)])
    key_grad, value_grad = call(
        pair_kernel,
        [rows_spec(0, two)] * 2 + [stack_spec(2, 0, two)] * 5
        + [pl.BlockSpec((1, 2, BLOCK, two * HD), lambda h: (0, 0, 0, h))] * 3,
        [(rows_spec(0, two), half_rows)] * 2,
        1,
        heads // two,
    )(flags, dk_b, dv_b, above, below, *returned, joint, *gots)
    whole = pl.BlockSpec((1, 2, BLOCK, width), lambda h: (1, 0, 0, 0))
    anywhere = pl.BlockSpec(memory_space=pl.ANY)
    attention, query_grad = call(
        root_kernel,
        [whole] * 3 + [anywhere] * 2,
        [(anywhere, half_rows)] * 2,
        1,
        1,
        input_output_aliases={4: 0, 5: 1},
        scratch_shapes=[pltpu.VMEM((2, BLOCK, width), BF16), pltpu.SemaphoreType.DMA((2,))],
    )(ends, joint, *gots, att_r, dq_r)
    return (attention[None], query_grad[None], key_grad[None], value_grad[None], sink_grad)


def solution(mesh):
    whole = P("dp", "ctx", "head")
    return jax.shard_map(
        device_body,
        mesh=mesh,
        in_specs=(whole, whole, whole, P("head"), P(), P("dp", None, None), whole),
        out_specs=(whole, whole, whole, whole, P("head")),
        check_vma=False,
    )
```

```python
import math

import jax
import jax.numpy as jnp
from jax import lax
from jax.experimental import pallas as pl
from jax.experimental.pallas import tpu as pltpu
from jax.sharding import PartitionSpec as P


HD = 128
BLOCK = 128
ROUNDS = 3
BITS = 5
CTX = 32
INTERPRET = False
F32 = jnp.float32
BF16 = jnp.bfloat16
SCALING = HD ** (-0.5)
LOG2E = math.log2(math.e)
EXP2 = SCALING * LOG2E
NT = (((1,), (1,)), ((), ()))
NN = (((1,), (0,)), ((), ()))
TN = (((0,), (0,)), ((), ()))


def dot(a, b, dims):
    return lax.dot_general(a, b, dims, preferred_element_type=F32)


def move(value, pairs):
    return lax.ppermute(value, "ctx", pairs)


def flip(value, bit):
    return move(value, [(i, i ^ (1 << bit)) for i in range(CTX)])


TREE = (
    (
        (((0, 0), (0, 3)),),
        (((0, 0), (0, 5)),),
    ),
    (
        (((0, 0), (0, 7)), ((0, 3), (0, 4)), ((0, 5), (0, 6))),
        (((0, 0), (1, 0)), ((0, 3), (1, 3)), ((0, 5), (1, 5))),
    ),
    (
        (
            ((0, 0), (0, 1)), ((0, 3), (0, 2)), ((1, 0), (1, 1)), ((1, 3), (1, 2)),
            ((0, 4), (1, 4)), ((0, 6), (1, 6)), ((0, 7), (1, 7)),
        ),
    ),
)


def tree_pairs(edges):
    pairs = [(a[0] * 16 + a[1] * 2, b[0] * 16 + b[1] * 2) for a, b in edges]
    return pairs + [(CTX - 1 - i, CTX - 1 - j) for i, j in pairs]


def member(place, devices):
    bits = sum(1 << i for i in devices)
    return (jnp.uint32(bits) >> place.astype(jnp.uint32)) & jnp.uint32(1) == 1


def routed(package, bit_place):
    return lax.switch(
        bit_place, [lambda value, bit=bit: flip(value, bit) for bit in range(BITS)], package
    )


def pick_kernel(place, partner, picks, k, v, info, pa, pb, pc):
    bits = []
    wanted = []
    for r in range(ROUNDS):
        mask = partner[r, 0]
        bits.append(sum((mask >= (1 << b)).astype(jnp.int32) for b in range(1, BITS)))
        wanted.append(picks[0, r, jnp.bitwise_xor(place[0], mask)])
    ranks = []
    for r in range(ROUNDS):
        ahead = [(bits[o] <= bits[r]) if o < r else (bits[o] < bits[r]) for o in range(ROUNDS) if o != r]
        ranks.append(sum(value.astype(jnp.int32) for value in ahead))
    for slot, out in enumerate((pa, pb, pc)):
        chosen = [(ranks[r] == slot).astype(jnp.int32) for r in range(ROUNDS)]
        block = sum(chosen[r] * wanted[r] for r in range(ROUNDS))
        info[slot] = sum(chosen[r] * bits[r] for r in range(ROUNDS))
        info[ROUNDS + slot] = block
        rows = pl.ds(pl.multiple_of(block * BLOCK, BLOCK), BLOCK)
        out[0] = k[rows]
        out[1] = v[rows]


def regular_kernel(
    flags, sink, q, g, k, v, prev, nxt, mine, other, ra, rb, rc,
    *refs, first_head,
):
    att, dq, dk_own, dv_own, d_prev, d_next, d_mine, d_other, d_ra, d_rb, d_rc, sink_out = refs[-12:]
    sink_h = sink[pl.program_id(0) + first_head] * (1.0 / SCALING)
    ends = (flags[0] == 1, flags[1] == 1)
    zero = jnp.zeros((BLOCK, HD), BF16)
    halves = (slice(0, BLOCK), slice(BLOCK, 2 * BLOCK))
    qq = q[...]
    gg = jnp.concatenate([jnp.where(ends[n], zero, g[halves[n]]) for n in range(2)], axis=0)
    k_shared = jnp.concatenate([mine[1], other[1], ra[0], rb[0], rc[0]], axis=0)
    v_shared = jnp.concatenate([mine[2], other[2], ra[1], rb[1], rc[1]], axis=0)
    k_line = jnp.concatenate([prev[0], k[...], nxt[0]], axis=0)
    v_line = jnp.concatenate([prev[1], v[...], nxt[1]], axis=0)
    near = [slice(n * BLOCK, (n + 3) * BLOCK) for n in range(2)]

    def joined(make):
        return jnp.concatenate([make(n) for n in range(2)], axis=0)

    def near_scores(n):
        s = dot(qq[halves[n]], k_line[near[n]], NT)
        parts = [s[:, j * BLOCK : (j + 1) * BLOCK] for j in range(3)]
        masked = 0 if n == 1 else 2
        parts[masked] = jnp.where(ends[1 - n], -jnp.inf, parts[masked])
        return jnp.concatenate(parts, axis=1)

    s_far = dot(qq, k_shared, NT)
    s_near = joined(near_scores)
    top = jnp.maximum(jnp.max(s_far, axis=1, keepdims=True), jnp.max(s_near, axis=1, keepdims=True))
    top = jnp.maximum(top, sink_h)
    e_far = jnp.exp2((s_far - top) * EXP2)
    e_near = jnp.exp2((s_near - top) * EXP2)
    sink_e = jnp.exp2((sink_h - top) * EXP2)
    total = sink_e + jnp.sum(e_far, axis=1, keepdims=True) + jnp.sum(e_near, axis=1, keepdims=True)
    inverse = 1.0 / total
    h_far = e_far.astype(BF16)
    h_near = e_near.astype(BF16)
    acc = dot(h_far, v_shared, NN) + joined(lambda n: dot(h_near[halves[n]], v_line[near[n]], NN))
    half = (acc * inverse).astype(BF16)
    att[...] = half
    delta = jnp.sum(gg.astype(F32) * half.astype(F32), axis=1, keepdims=True)
    sink_sum = jnp.sum(sink_e * inverse * delta, axis=0, keepdims=True)
    sink_out[0] = jnp.broadcast_to(sink_sum, (8, HD))
    p_far = e_far * inverse
    p_near = e_near * inverse
    ds_far = (p_far * (dot(gg, v_shared, NT) - delta)).astype(BF16)
    dp_near = joined(lambda n: dot(gg[halves[n]], v_line[near[n]], NT))
    ds_near = (p_near * (dp_near - delta)).astype(BF16)
    p_far = p_far.astype(BF16)
    p_near = p_near.astype(BF16)
    back = dot(ds_far, k_shared, NN) + joined(lambda n: dot(ds_near[halves[n]], k_line[near[n]], NN))
    dq[...] = (back * SCALING).astype(BF16)
    for part, far, close, rows, scale, own in (
        (0, ds_far, ds_near, qq, SCALING, dk_own), (1, p_far, p_near, gg, 1.0, dv_own)
    ):
        shared = dot(far, rows, TN) * scale
        for j, out in enumerate((d_mine, d_other, d_ra, d_rb, d_rc)):
            out[part] = shared[j * BLOCK : (j + 1) * BLOCK].astype(BF16)
        low, high = [dot(close[halves[n]], rows[halves[n]], TN) * scale for n in range(2)]
        d_prev[part] = low[:BLOCK].astype(BF16)
        d_next[part] = high[2 * BLOCK :].astype(BF16)
        own[...] = low[BLOCK:] + high[: 2 * BLOCK]


def head_slices(ref):
    return [slice(h * HD, (h + 1) * HD) for h in range(ref.shape[-1] // HD)]


def in_order(first, second, swap):
    return jnp.concatenate([jnp.where(swap, second, first), jnp.where(swap, first, second)], axis=0)


def stats_kernel(flags, k, v, mine, other, stats):
    swap = flags[2] == 1
    lanes_of = head_slices(k)
    for h, lanes in enumerate(lanes_of):
        row = pl.ds(pl.program_id(0) * len(lanes_of) + h, 1)
        gq = in_order(mine[0, :, lanes], other[0, :, lanes], swap)
        gg = in_order(mine[3, :, lanes], other[3, :, lanes], swap)
        s = dot(k[:, lanes], gq, NT)
        top = jnp.max(s, axis=0, keepdims=True)
        e = jnp.exp2((s - top) * EXP2)
        dp = dot(v[:, lanes], gg, NT)
        stats[0, row] = top * SCALING
        stats[1, row] = jnp.sum(e, axis=0, keepdims=True)
        stats[2, row] = jnp.sum(e * dp, axis=0, keepdims=True)


def global_kernel(
    flags, sink, k, v, mine, other, stats, dk_in, dv_in,
    d_mine, d_other, dk_out, dv_out, sink_out,
):
    swap = flags[2] == 1
    lanes_of = head_slices(k)
    for h, lanes in enumerate(lanes_of):
        number = pl.program_id(0) * len(lanes_of) + h
        row = pl.ds(number, 1)
        sink_h = sink[number]
        local = stats[0, row]
        top = jnp.maximum(local, sink_h)
        factor = jnp.exp(local - top)
        sink_e = jnp.exp(sink_h - top)
        total = sink_e + stats[1, row] * factor
        lse = (top + jnp.log(total)) * LOG2E
        delta = stats[2, row] * factor / total
        sink_out[h] = jnp.broadcast_to(jnp.sum(sink_e / total * delta, axis=1, keepdims=True), (8, HD))
        lse = jnp.where(swap, jnp.concatenate([lse[:, BLOCK:], lse[:, :BLOCK]], axis=1), lse)
        delta = jnp.where(swap, jnp.concatenate([delta[:, BLOCK:], delta[:, :BLOCK]], axis=1), delta)
        gq = jnp.concatenate([mine[0, :, lanes], other[0, :, lanes]], axis=0)
        gg = jnp.concatenate([mine[3, :, lanes], other[3, :, lanes]], axis=0)
        kk = k[:, lanes]
        vv = v[:, lanes]
        p = jnp.exp2(dot(kk, gq, NT) * EXP2 - lse)
        ph = p.astype(BF16)
        ds = (p * (dot(vv, gg, NT) - delta)).astype(BF16)
        acc = dot(ph, vv, TN).astype(BF16)
        dq = (dot(ds, kk, TN) * SCALING).astype(BF16)
        d_mine[0, :, lanes] = acc[:BLOCK]
        d_mine[1, :, lanes] = dq[:BLOCK]
        d_other[0, :, lanes] = acc[BLOCK:]
        d_other[1, :, lanes] = dq[BLOCK:]
        dk_out[:, lanes] = dk_in[:, lanes] + dot(ds, gq, NN) * SCALING
        dv_out[:, lanes] = dv_in[:, lanes] + dot(ph, gg, NN)


def pair_kernel(flags, dk_in, dv_in, above, below, ra, rb, rc, own, ga, gb, dk, dv):
    for n in range(2):
        rows = slice(n * BLOCK, (n + 1) * BLOCK)
        is_root = flags[n] == 1
        edge = below if n == 0 else above
        for part, (out, first) in enumerate(((dk, dk_in), (dv, dv_in))):
            value = first[rows] + edge[part].astype(F32)
            root = sum(ref[0, part].astype(F32) for ref in (own, ga, gb))
            value = value + jnp.where(is_root, root, 0.0)
            for r, back in enumerate((ra, rb, rc)):
                value = value + jnp.where(flags[2 + r] == n, back[part].astype(F32), 0.0)
            out[rows] = value.astype(BF16)


def root_kernel(flags, own, ga, gb, att_in, dq_in, att, dq, rows, sems):
    del att_in, dq_in
    is_last = flags[1] == 1

    @pl.when((flags[0] == 1) | is_last)
    def _():
        rows[...] = sum(ref[0].astype(F32) for ref in (own, ga, gb)).astype(BF16)
        start = pl.multiple_of(jnp.where(is_last, BLOCK, 0), BLOCK)
        copies = [
            pltpu.make_async_copy(rows.at[i], out.at[pl.ds(start, BLOCK)], sems.at[i])
            for i, out in enumerate((att, dq))
        ]
        for copy in copies:
            copy.start()
        for copy in copies:
            copy.wait()


def rows_spec(first=0, group=1):
    return pl.BlockSpec((2 * BLOCK, group * HD), lambda h: (0, h + first))


def stack_spec(depth, first=0, group=1):
    return pl.BlockSpec((depth, BLOCK, group * HD), lambda h: (0, 0, h + first))


def stat_spec(count, width, first=0, group=1):
    return pl.BlockSpec((group, count, width), lambda h: (h + first, 0, 0))


def smem_spec():
    return pl.BlockSpec(memory_space=pltpu.SMEM)


def shaped(shape, dtype):
    return jax.ShapeDtypeStruct(shape, dtype)


def add_half(a, b):
    return (a.astype(F32) + b.astype(F32)).astype(BF16)


def merge(a, b):
    top = jnp.maximum(a[:1], b[:1])
    summed = a * jnp.exp(a[:1] - top) + b * jnp.exp(b[:1] - top)
    return jnp.where(lax.broadcasted_iota(jnp.int32, a.shape, 0) == 0, top, summed)


PARTS = ((0, 3), (3, 3), (6, 2))
STAT_BITS = (3, 2, 4, 1, 0)
FETCH_SLOTS = (1, 0, 2)
BACK_SLOTS = (0, 2, 1)


def device_body(queries, key_rows, value_rows, sink_logits, partner, block_pick, out_grad):
    q, k, v, g = queries[0], key_rows[0], value_rows[0], out_grad[0]
    tokens, width = q.shape
    heads = width // HD
    two = math.gcd(heads, 2)
    four = math.gcd(heads, 4)
    place = lax.axis_index("ctx")
    is_first = (place == 0).astype(jnp.int32)
    is_last = (place == CTX - 1).astype(jnp.int32)

    def call(kernel, ins, outs, scalars=0, grid=None, **more):
        return lambda *operands: pl.pallas_call(
            kernel,
            grid=(heads if grid is None else grid,),
            in_specs=[smem_spec()] * scalars + ins,
            out_specs=[spec for spec, _ in outs],
            out_shape=[shape for _, shape in outs],
            interpret=INTERPRET,
            **more,
        )(*operands)

    heads_of = jnp.stack([array[:BLOCK] for array in (q, k, v, g)])
    tails_of = jnp.stack([array[tokens - BLOCK :] for array in (q, k, v, g)])
    mine = jnp.where(place == CTX - 1, tails_of, heads_of)
    mine, partner, block_pick = lax.optimization_barrier((mine, partner, block_pick))
    group = pl.BlockSpec((2 * BLOCK, width), lambda h: (0, 0))
    package = pl.BlockSpec((2, BLOCK, width), lambda h: (0, 0, 0))
    info, *packages = call(
        pick_kernel,
        [group] * 2,
        [(smem_spec(), shaped((2 * ROUNDS,), jnp.int32))]
        + [(package, shaped((2, BLOCK, width), BF16))] * ROUNDS,
        3,
        1,
    )(place[None].astype(jnp.int32), partner, block_pick, k, v)
    bit_places = info[:ROUNDS]
    wanted = info[ROUNDS:]

    up = [(i, i + 1) for i in range(CTX - 1)]
    down = [(i + 1, i) for i in range(CTX - 1)]
    low_pair = jnp.stack([k[:BLOCK], v[:BLOCK]])
    high_pair = jnp.stack([k[tokens - BLOCK :], v[tokens - BLOCK :]])
    prev = move(high_pair, up)
    nxt = move(low_pair, down)
    fetched = [None] * ROUNDS
    for step, stage in enumerate(TREE):
        gots = [move(mine, tree_pairs(edges)) for edges in stage]
        slot = FETCH_SLOTS[step]
        fetched[slot] = routed(packages[slot], bit_places[slot])
        for edges, got in zip(stage, gots):
            mine = jnp.where(member(place, [j for _, j in tree_pairs(edges)]), got, mine)
    other = flip(mine, 0)

    ends = jnp.stack([is_first, is_last, place & 1])
    stats_shape = shaped((3, heads, 2 * BLOCK), F32)
    stats_spec = pl.BlockSpec((3, heads, 2 * BLOCK), lambda h: (0, 0, 0))
    (stats,) = call(
        stats_kernel,
        [rows_spec(0, four)] * 2 + [stack_spec(4, 0, four)] * 2,
        [(stats_spec, stats_shape)],
        1,
        heads // four,
    )(ends, k, v, mine, other)
    for bit in STAT_BITS:
        arrived = flip(stats, bit)
        stats = merge(stats, arrived)

    pair = shaped((2, BLOCK, width), BF16)
    half_rows = shaped((tokens, width), BF16)
    full_rows = shaped((tokens, width), F32)
    shapes = [half_rows] * 2 + [full_rows] * 2 + [pair] * 7 + [shaped((heads, 8, HD), F32)]
    inputs = (ends, sink_logits, q, g, k, v, prev, nxt, mine, other, *fetched)
    kept = []
    parts = PARTS if heads == 8 else ((0, heads),)
    for first, count in parts:
        specs = [rows_spec(first)] * 4 + [stack_spec(2, first)] * 7 + [stat_spec(8, HD, first)]
        kept = call(
            lambda *refs, first=first: regular_kernel(*refs, first_head=first),
            [rows_spec(first)] * 4 + [stack_spec(2, first)] * 2 + [stack_spec(4, first)] * 2
            + [stack_spec(2, first)] * 3 + [pl.BlockSpec(memory_space=pl.ANY)] * len(kept),
            list(zip(specs, shapes)),
            2,
            count,
            input_output_aliases={len(inputs) + i: i for i in range(len(kept))},
        )(*inputs, *kept)
    (att_r, dq_r, dk_a, dv_a, d_prev, d_next, kv_mine, kv_other, *d_random, sink_part) = kept

    (aq_mine, aq_other, dk_b, dv_b, global_sink) = call(
        global_kernel,
        [rows_spec(0, two)] * 2 + [stack_spec(4, 0, two)] * 2 + [stats_spec]
        + [rows_spec(0, two)] * 2,
        [(stack_spec(2, 0, two), pair)] * 2 + [(rows_spec(0, two), full_rows)] * 2
        + [(stat_spec(8, HD, 0, two), shaped((heads, 8, HD), F32))],
        2,
        heads // two,
        input_output_aliases={7: 2, 8: 3},
    )(ends, sink_logits, k, v, mine, other, stats, dk_a, dv_a)

    above = move(d_prev, down)
    below = move(d_next, up)
    sink_row = sink_part
    kv_got = flip(kv_other, 0)
    sink_row = sink_row + flip(sink_row, 0)
    sink_row = sink_row + flip(sink_row, 1)
    aq_got = flip(aq_other, 0)
    sink_row = sink_row + flip(sink_row, 2)
    joint = jnp.stack([add_half(kv_mine, kv_got), add_half(aq_mine, aq_got)])
    returned = [None] * ROUNDS
    docs = lax.axis_size("dp")

    def flip_docs(value, bit):
        if docs < 4 and bit:
            return jnp.zeros_like(value)
        return lax.ppermute(value, "dp", [(i, i ^ (1 << bit)) for i in range(docs)])

    for step, stage in enumerate(TREE[::-1]):
        gots = [move(joint, [(j, i) for i, j in tree_pairs(edges)]) for edges in stage]
        sink_got = flip(sink_row, step + 3) if step < 2 else flip_docs(sink_row, 0)
        slot = BACK_SLOTS[step]
        returned[slot] = routed(d_random[slot], bit_places[slot])
        sink_row = sink_row + sink_got
        if step < 2:
            sink_row = sink_row if step == 0 else sink_row + global_sink
            joint = (joint.astype(F32) + sum(got.astype(F32) for got in gots)).astype(BF16)
    sink_row = sink_row + flip_docs(sink_row, 1)
    sink_grad = -sink_row[:, 0, 0] / math.sqrt(docs * CTX * tokens)

    flags = jnp.concatenate([ends[:2], wanted.astype(jnp.int32)])
    key_grad, value_grad = call(
        pair_kernel,
        [rows_spec(0, two)] * 2 + [stack_spec(2, 0, two)] * 5
        + [pl.BlockSpec((1, 2, BLOCK, two * HD), lambda h: (0, 0, 0, h))] * 3,
        [(rows_spec(0, two), half_rows)] * 2,
        1,
        heads // two,
    )(flags, dk_b, dv_b, above, below, *returned, joint, *gots)
    whole = pl.BlockSpec((1, 2, BLOCK, width), lambda h: (1, 0, 0, 0))
    anywhere = pl.BlockSpec(memory_space=pl.ANY)
    attention, query_grad = call(
        root_kernel,
        [whole] * 3 + [anywhere] * 2,
        [(anywhere, half_rows)] * 2,
        1,
        1,
        input_output_aliases={4: 0, 5: 1},
        scratch_shapes=[pltpu.VMEM((2, BLOCK, width), BF16), pltpu.SemaphoreType.DMA((2,))],
    )(ends, joint, *gots, att_r, dq_r)
    return (attention[None], query_grad[None], key_grad[None], value_grad[None], sink_grad)


def solution(mesh):
    whole = P("dp", "ctx", "head")
    return jax.shard_map(
        device_body,
        mesh=mesh,
        in_specs=(whole, whole, whole, P("head"), P(), P("dp", None, None), whole),
        out_specs=(whole, whole, whole, whole, P("head")),
        check_vma=False,
    )
```
